32 devices in a mesh: chan: 8 (over y, x, core), band: 4 (over z).
Axes of the slice: x: 2, y: 2, z: 4, core: 2. Of those that a mesh axis runs over, the one named last changes fastest.
Arguments:
- spectra: bfloat16 [96, 2048, 384], P('band', 'chan')
- half_width: int32 [2048], P('chan'), may hold values from 4 to 12
- partner: int32 [2, 8], replicated, may hold values from 0 to 7, as said below
Outputs:
- cross: bfloat16 [3, 96, 2048, 512], P(None, 'band', 'chan')
The draws below stay inside these ranges and needn't reach their ends.
Inputs may be any that keep to these rules, and one draw needn't show every extreme that they name: Each row pairs the blocks: partner[r, partner[r, a]] = a and partner[r, a] != a; no two rows pair the same two blocks.
All inputs are finite; a program needn't handle non-finite values.
Results may differ from the reference program's by a relative error of at most 0.0056.
Values may be sent and summed in bfloat16 or wider, within the bound.
No kernel may reach another device: no remote copies, remote signals or barrier semaphores. Data moves between devices by JAX's collectives and lax.ppermute only.
A program may use at most 128 MiB of HBM per device.

```python
import jax
import jax.numpy as jnp
from jax import lax

CB = 256
W = 192
HMIN = 4
HMAX = 12
ROUNDS = 2
NBLK = 8
NCH = 2048
NF = 96


def draw_spectra(key, part):
    keys = jax.random.split(jax.random.fold_in(key, 11), 4)
    base = jax.random.normal(keys[0], (NF, NCH, 2 * W))
    chan_scale = jnp.exp(jax.random.uniform(keys[1], (1, NCH, 1), minval=0.0, maxval=2.3))
    bin_scale = jnp.exp(jax.random.uniform(keys[2], (NF, 1, 1), minval=0.0, maxval=2.3))
    window_scale = jnp.exp(jax.random.uniform(keys[3], (1, 1, W), minval=0.0, maxval=2.3))
    window_scale = jnp.concatenate([window_scale, window_scale], axis=2)
    return (base * chan_scale * bin_scale * window_scale).astype(jnp.bfloat16)


def draw_half_width(key, part):
    values = jax.random.randint(jax.random.fold_in(key, 12), (NCH,), HMIN, HMAX + 1)
    return values.at[0].set(HMAX).at[1].set(HMIN).astype(jnp.int32)


def draw_partner(key, part):
    keys = jax.random.split(jax.random.fold_in(key, 13), 2)
    labels = jax.random.permutation(keys[0], NBLK).astype(jnp.int32)
    inverse = jnp.zeros((NBLK,), jnp.int32).at[labels].set(jnp.arange(NBLK, dtype=jnp.int32))
    chosen = jax.random.permutation(keys[1], NBLK - 1)[:ROUNDS].astype(jnp.int32)
    label = labels[None, :]
    which = chosen[:, None]
    mirrored = jnp.mod(2 * which - label, NBLK - 1)
    paired = jnp.where(label == NBLK - 1, which, jnp.where(label == which, NBLK - 1, mirrored))
    return inverse[paired].astype(jnp.int32)


def setup_inputs(seed: int = 0) -> dict:
    key_list = jax.random.split(jax.random.key(seed), 4)
    return {
        "spectra": draw_spectra(jax.random.fold_in(key_list[3], 71), 0),
        "half_width": draw_half_width(jax.random.fold_in(key_list[3], 71), 0),
        "partner": draw_partner(jax.random.fold_in(key_list[3], 71), 0),
    }


def whiten(spectra, half_width):
    raw = spectra.astype(jnp.float32)
    power = lax.optimization_barrier(jnp.sum(raw * raw, axis=2))
    padded = jnp.pad(power, ((HMAX, HMAX), (0, 0)))
    present = jnp.pad(jnp.ones((NF, 1), jnp.float32), ((HMAX, HMAX), (0, 0)))
    total = jnp.zeros((NF, NCH), jnp.float32)
    count = jnp.zeros((NF, NCH), jnp.float32)
    for offset in range(-HMAX, HMAX + 1):
        inside = (abs(offset) <= half_width).astype(jnp.float32)[None, :]
        total = total + padded[HMAX + offset:HMAX + offset + NF] * inside
        count = count + present[HMAX + offset:HMAX + offset + NF] * inside
    scale = lax.rsqrt(total / (2.0 * W * count) + 1e-06)
    return (raw * scale[:, :, None]).astype(jnp.bfloat16)

def pair_block(own, other):
    left = own.astype(jnp.float32)
    right_raw = other.astype(jnp.float32)
    turned = jnp.concatenate([-right_raw[:, :, W:], right_raw[:, :, :W]], axis=2)
    right = jnp.concatenate([right_raw, turned], axis=1)
    product = jnp.einsum('fcw,fdw->fcd', left, right, precision=lax.Precision.HIGHEST)
    return (product * (1.0 / W)).astype(jnp.bfloat16)

def reference(spectra, half_width, partner):
    white = whiten(spectra, half_width)

    def one_block(block):
        own = lax.dynamic_slice_in_dim(white, (block * CB).astype(jnp.int32), CB, 1)
        results = [pair_block(own, own)]
        for step in range(ROUNDS):
            start = (partner[step, block] * CB).astype(jnp.int32)
            other = lax.dynamic_slice_in_dim(white, start, CB, 1)
            results.append(pair_block(own, other))
        return jnp.stack(results)
    blocks = lax.map(one_block, jnp.arange(NBLK, dtype=jnp.int32))
    return jnp.transpose(blocks, (1, 2, 0, 3, 4)).reshape(ROUNDS + 1, NF, NCH, 2 * CB)
```

```python
import functools

import jax
import jax.numpy as jnp
from jax import lax
from jax.experimental import pallas as pl
from jax.experimental.pallas import tpu as pltpu
from jax.sharding import PartitionSpec as P


HMAX = 12
ROUNDS = 2
CORE = 1
AXIS_X = 2
AXIS_Y = 4


def padded_2(cells, sides, width):
    for axis, dim in sides:
        count = lax.axis_size(axis)
        ends = count - 1
        head = lax.slice_in_dim(cells, 0, width, axis=dim)
        tail = lax.slice_in_dim(cells, cells.shape[dim] - width, cells.shape[dim], axis=dim)
        cells = jnp.concatenate(
            [
                lax.ppermute(tail, axis, [(i, (i + 1) % count) for i in range(ends)]),
                cells,
                lax.ppermute(head, axis, [((i + 1) % count, i) for i in range(ends)]),
            ],
            axis=dim,
        )
    return cells


def pair_block(own, other, windows):
    turned = jnp.concatenate([-other[:, :, windows:], other[:, :, :windows]], axis=2)
    right = jnp.concatenate([other, turned], axis=1)
    product = jnp.einsum("fcw,fdw->fcd", own, right, preferred_element_type=jnp.float32)
    return (product * (1.0 / windows)).astype(jnp.bfloat16)


def whitening_scale(spectra, half_width):
    bins, chans, columns = spectra.shape
    windows = columns // 2
    raw = spectra.astype(jnp.float32)
    power = jnp.sum(raw * raw, axis=2)
    padded = padded_2(power, (("band", 0),), HMAX)
    first = lax.axis_index("band") * bins - HMAX
    position = first + jnp.arange(bins + 2 * HMAX, dtype=jnp.int32)
    present = ((position >= 0) & (position < bins * lax.axis_size("band"))).astype(jnp.float32)[
        :, None
    ]
    total = jnp.zeros((bins, chans), jnp.float32)
    count = jnp.zeros((bins, chans), jnp.float32)
    for offset in range(-HMAX, HMAX + 1):
        inside = (abs(offset) <= half_width).astype(jnp.float32)[None, :]
        total = total + padded[HMAX + offset : HMAX + offset + bins] * inside
        count = count + present[HMAX + offset : HMAX + offset + bins] * inside
    return lax.rsqrt(total / (2.0 * windows * count) + 1e-06)


def whitened(raw, scale):
    return (raw.astype(jnp.float32) * scale[..., None]).astype(jnp.bfloat16)


def general_body(spectra, half_width, partner):
    bins, chans, columns = spectra.shape
    windows = columns // 2
    white = whitened(spectra, whitening_scale(spectra, half_width))
    blocks = lax.axis_size("chan")
    piece = chans // blocks
    sectioned = white.reshape(bins, blocks, piece, columns)
    results = [pair_block(white, white, windows)]
    for step in range(ROUNDS):
        held = lax.all_to_all(sectioned, "chan", split_axis=1, concat_axis=1, tiled=True)
        chosen = jnp.take(held, partner[step], axis=1)
        other = lax.all_to_all(chosen, "chan", split_axis=1, concat_axis=1, tiled=True)
        results.append(pair_block(white, other.reshape(bins, chans, columns), windows))
    return jnp.stack(results)


def swap(values, offset):
    return lax.ppermute(values, "chan", [(i, i ^ offset) for i in range(lax.axis_size("chan"))])


def line_of(first):
    return (0, CORE, first, first | CORE)


SEND, TAKE, GIVE, ROUTE = 0, 4, 6, 8


def route_base(first):
    return 8 if first == AXIS_X else 8 + ROUTE


def route_kernel(devices, device_ref, partner_ref, out_ref):
    def needed(sender, first, second):
        receiver = sender ^ second
        wanted = [
            partner_ref[r, who] for r in range(ROUNDS) for who in (receiver, receiver ^ CORE)
        ]
        need = []
        for place in line_of(first):
            hit = (sender ^ wanted[0]) == place
            for want in wanted[1:]:
                hit = hit | ((sender ^ want) == place)
            need.append(hit.astype(jnp.int32))
        return need

    def slots(need):
        slot = [jnp.int32(0)]
        for flag in need[:-1]:
            slot.append(slot[-1] + flag)
        return slot

    device = device_ref[0]
    for place in range(8 + 2 * ROUTE):
        out_ref[place] = 0
    for which, (first, second) in enumerate(((AXIS_X, AXIS_Y), (AXIS_Y, AXIS_X))):
        most = jnp.int32(0)
        for chip in range(0, devices, 2):
            need = needed(jnp.int32(chip), first, second)
            most = jnp.maximum(most, need[0] + need[1] + need[2] + need[3])
        out_ref[which] = most
        base = route_base(first)
        need = needed(device, first, second)
        slot = slots(need)
        for s in range(4):
            value = jnp.int32(0)
            for place in range(4):
                value = value + place * need[place] * (slot[place] == s).astype(jnp.int32)
            out_ref[base + SEND + s] = value
        slot = slots(needed(device ^ second, first, second))
        for r in range(ROUNDS):
            for at, who in ((TAKE, device), (GIVE, device ^ CORE)):
                offset = device ^ partner_ref[r, who]
                value = jnp.int32(0)
                for place, bits in enumerate(line_of(first)):
                    near = (offset == bits).astype(jnp.int32)
                    far = (offset == (bits | second)).astype(jnp.int32)
                    value = value + near * place + far * (4 + slot[place])
                out_ref[base + at + r] = value


def routes(device, partner):
    smem = pl.BlockSpec(memory_space=pltpu.SMEM)
    return pl.pallas_call(
        functools.partial(route_kernel, partner.shape[1]),
        out_shape=jax.ShapeDtypeStruct((8 + 2 * ROUTE,), jnp.int32),
        in_specs=[smem, smem],
        out_specs=smem,
        name="route",
    )(device.reshape(1), partner)


def line_kernel(base, slots, route, at, own, sister, near, far, scale, line, sent):
    for b in range(own.shape[0]):
        columns = jnp.transpose(scale[b])
        for place, ref in enumerate((own, sister, near, far)):
            raw = ref[b].astype(jnp.float32)
            line[place, b] = (raw * columns[:, place : place + 1]).astype(jnp.bfloat16)
    for s in range(slots):
        sent[s] = line[route[base + SEND + s]]


def line_blocks(first, slots, route, at, own, sister, near, far, scale):
    part, chans, columns = far.shape
    step = 1

    def spec(place):
        return pl.BlockSpec(
            (pl.Element(step), pl.Element(chans), pl.Element(columns)),
            lambda i, route, at: (at[place] + i * step, 0, 0),
        )

    return pl.pallas_call(
        functools.partial(line_kernel, route_base(first), slots),
        out_shape=(
            jax.ShapeDtypeStruct((4, part, chans, columns), jnp.bfloat16),
            jax.ShapeDtypeStruct((slots, part, chans, columns), jnp.bfloat16),
        ),
        grid_spec=pltpu.PrefetchScalarGridSpec(
            num_scalar_prefetch=2,
            grid=(part // step,),
            in_specs=[
                spec(0),
                spec(2),
                spec(1),
                pl.BlockSpec((step, chans, columns), lambda i, route, at: (i, 0, 0)),
                pl.BlockSpec(
                    (pl.Element(step), pl.Element(8), pl.Element(chans)),
                    lambda i, route, at: (at[3] + i * step, 0, 0),
                ),
            ],
            out_specs=[
                pl.BlockSpec((4, step, chans, columns), lambda i, route, at: (0, i, 0, 0)),
                pl.BlockSpec((slots, step, chans, columns), lambda i, route, at: (0, i, 0, 0)),
            ],
        ),
        cost_estimate=pl.CostEstimate(
            flops=8 * part * chans * columns,
            bytes_accessed=2 * part * chans * columns * (8 + slots),
            transcendentals=0,
        ),
        name="line",
    )(route, at, own, sister, near, far, scale)


def give_kernel(base, route, line, got, out):
    place = route[base + GIVE + pl.program_id(0)]

    @pl.when(place < 4)
    def _():
        out[...] = line[...]

    @pl.when(place >= 4)
    def _():
        out[...] = got[...]


def given(first, route, line, got):
    part, chans, columns = line.shape[1:]
    base = route_base(first)
    shape = (1, part, chans, columns)
    return pl.pallas_call(
        functools.partial(give_kernel, base),
        out_shape=jax.ShapeDtypeStruct((ROUNDS, part, chans, columns), jnp.bfloat16),
        grid_spec=pltpu.PrefetchScalarGridSpec(
            num_scalar_prefetch=1,
            grid=(ROUNDS,),
            in_specs=[
                pl.BlockSpec(shape, lambda r, route: (jnp.minimum(route[base + GIVE + r], 3), 0, 0, 0)),
                pl.BlockSpec(
                    shape, lambda r, route: (jnp.maximum(route[base + GIVE + r] - 4, 0), 0, 0, 0)
                ),
            ],
            out_specs=pl.BlockSpec(shape, lambda r, route: (r, 0, 0, 0)),
        ),
        cost_estimate=pl.CostEstimate(
            flops=0, bytes_accessed=12 * part * chans * columns, transcendentals=0
        ),
        name="give",
    )(route, line, got)


def multiply(own, turned, other, out_ref, at, bin_at, windows):
    contract = (((1,), (1,)), ((), ()))
    chans = own.shape[0]
    re = lax.dot_general(own, other, contract, preferred_element_type=jnp.float32)
    im = lax.dot_general(turned, other, contract, preferred_element_type=jnp.float32)
    out_ref[at, bin_at, :, :chans] = (re * (1.0 / windows)).astype(jnp.bfloat16)
    out_ref[at, bin_at, :, chans:] = (im * (1.0 / windows)).astype(jnp.bfloat16)


def own_kernel(own, turned, out_ref):
    for b in range(own.shape[0]):
        multiply(own[b], turned[b], own[b], out_ref, 0, b, own.shape[2] // 2)


def own_products(own, turned):
    bins, chans, columns = own.shape
    step = 3
    spec = pl.BlockSpec((step, chans, columns), lambda i: (i, 0, 0))
    return pl.pallas_call(
        own_kernel,
        out_shape=jax.ShapeDtypeStruct((1 + ROUNDS, bins, chans, 2 * chans), jnp.bfloat16),
        grid=(bins // step,),
        in_specs=[spec, spec],
        out_specs=pl.BlockSpec((1, step, chans, 2 * chans), lambda i: (0, i, 0, 0)),
        cost_estimate=pl.CostEstimate(
            flops=4 * bins * chans * chans * columns,
            bytes_accessed=4 * bins * chans * (columns + chans),
            transcendentals=0,
        ),
        name="own_products",
    )(own, turned)


def here_kernel(base, route, at, own, turned, line0, got0, line1, got1, result, out_ref):
    for b in range(own.shape[0]):
        for r, (line, got) in enumerate(((line0, got0), (line1, got1))):
            near = route[base + TAKE + r] < 4
            other = jnp.where(near, line[0, b], got[0, b])
            multiply(own[b], turned[b], other, out_ref, r, b, own.shape[2] // 2)


def there_kernel(route, at, own, turned, other, result, out_ref):
    for b in range(own.shape[0]):
        for r in range(ROUNDS):
            multiply(own[b], turned[b], other[r, b], out_ref, r, b, own.shape[2] // 2)


def pair_products(kernel, route, at, own, turned, others, other_specs, part, step, result):
    _, chans, columns = own.shape
    own_spec = pl.BlockSpec(
        (pl.Element(step), pl.Element(chans), pl.Element(columns)),
        lambda i, route, at: (at[0] + i * step, 0, 0),
    )
    return pl.pallas_call(
        kernel,
        out_shape=jax.ShapeDtypeStruct(result.shape, result.dtype),
        grid_spec=pltpu.PrefetchScalarGridSpec(
            num_scalar_prefetch=2,
            grid=(part // step,),
            in_specs=[own_spec, own_spec, *other_specs, pl.BlockSpec(memory_space=pl.ANY)],
            out_specs=pl.BlockSpec(
                (pl.Element(ROUNDS), pl.Element(step), pl.Element(chans), pl.Element(2 * chans)),
                lambda i, route, at: (1, at[0] + i * step, 0, 0),
            ),
        ),
        input_output_aliases={4 + len(others): 0},
        cost_estimate=pl.CostEstimate(
            flops=8 * part * chans * chans * columns,
            bytes_accessed=8 * part * chans * (columns + chans),
            transcendentals=0,
        ),
    )(route, at, own, turned, *others, result)


def here_products(first, route, at, own, turned, line, got, result):
    part, chans, columns = line.shape[1:]
    base = route_base(first)
    step = 1
    shape = (1, step, chans, columns)
    specs, others = [], []
    for r in range(ROUNDS):
        specs.append(
            pl.BlockSpec(
                shape,
                lambda i, route, at, r=r: (jnp.minimum(route[base + TAKE + r], 3), i, 0, 0),
            )
        )
        specs.append(
            pl.BlockSpec(
                shape,
                lambda i, route, at, r=r: (jnp.maximum(route[base + TAKE + r] - 4, 0), i, 0, 0),
            )
        )
        others += [line, got]
    kernel = functools.partial(here_kernel, base)
    return pair_products(kernel, route, at, own, turned, others, specs, part, step, result)


def there_products(route, at, own, turned, other, result):
    part, chans, columns = other.shape[1:]
    step = 1
    specs = [pl.BlockSpec((ROUNDS, step, chans, columns), lambda i, route, at: (0, i, 0, 0))]
    return pair_products(there_kernel, route, at, own, turned, [other], specs, part, step, result)


def plan_of(along_x):
    pieces = []
    x_sizes, y_sizes = along_x
    start_x, start_y = 0, 2 * sum(x_sizes)
    for place in range(max(len(x_sizes), len(y_sizes))):
        if place < len(x_sizes):
            pieces.append((start_x, x_sizes[place], AXIS_X))
            start_x += 2 * x_sizes[place]
        if place < len(y_sizes):
            pieces.append((start_y, y_sizes[place], AXIS_Y))
            start_y += 2 * y_sizes[place]
    return pieces


def exchange(slots, sizes, spectra, half_width, route, device):
    _, _, columns = spectra.shape
    windows = columns // 2
    core = device & CORE
    plan = plan_of(sizes)
    near = []
    for start, part, first in plan:
        near.append(swap(spectra[start : start + 2 * part], first))
    sister = [
        lax.dynamic_slice_in_dim(spectra, start + (1 - core) * part, part)
        for start, part, first in plan
    ]
    sister = swap(jnp.concatenate(sister), CORE)
    scale = whitening_scale(spectra, half_width)
    pair = jnp.stack([scale, swap(scale, CORE)])
    scales = {}
    for first in (AXIS_X, AXIS_Y):
        parts = jnp.concatenate([pair, swap(pair, first), jnp.zeros((4,) + scale.shape)])
        scales[first] = jnp.swapaxes(parts, 0, 1)
    own_white = whitened(spectra, scale)
    turned = jnp.concatenate([own_white[:, :, windows:], -own_white[:, :, :windows]], axis=2)
    result = own_products(own_white, turned)
    pools = []
    shared_at = 0
    for n, (start, part, first) in enumerate(plan):
        far = lax.dynamic_slice_in_dim(near[n], (1 - core) * part, part)
        far = swap(far, CORE)
        mine = start + core * part
        at = jnp.stack([mine, core * part, jnp.int32(shared_at), mine])
        shared_at += part
        line, sent = line_blocks(
            first, slots[first], route, at, spectra, sister, near[n], far, scales[first]
        )
        got = swap(sent, AXIS_X + AXIS_Y - first)
        pools.append((line, got))
    for pair in range(0, len(plan), 2):
        gifts = []
        for n in range(pair, min(pair + 2, len(plan))):
            start, part, first = plan[n]
            line, got = pools[n]
            gift = given(first, route, line, got)
            gifts.append(swap(gift, CORE))
            at = (start + core * part).reshape(1)
            result = here_products(first, route, at, own_white, turned, line, got, result)
        for n in range(pair, min(pair + 2, len(plan))):
            start, part, first = plan[n]
            at = (start + (1 - core) * part).reshape(1)
            result = there_products(route, at, own_white, turned, gifts[n - pair], result)
    return result


CASES = [
    (2, ((4, 2), (4, 2))),
    (3, ((4, 2), (4, 2))),
    (4, ((4, 2), (4, 2))),
]


def paired_body(spectra, half_width, partner):
    device = lax.axis_index("chan").astype(jnp.int32)
    route = routes(device, partner)
    most = jnp.maximum(route[0], route[1])
    choices = [
        functools.partial(exchange, {AXIS_X: slots, AXIS_Y: slots}, sizes)
        for slots, sizes in CASES
    ]
    return lax.switch(jnp.clip(most - 2, 0, 2), choices, spectra, half_width, route, device)


def solution(mesh):
    placed = (P("band", "chan", None), P("chan"), P())
    paired = mesh.shape["chan"] == 8
    return jax.shard_map(
        paired_body if paired else general_body,
        mesh=mesh,
        in_specs=placed,
        out_specs=P(None, "band", "chan", None),
        check_vma=False,
    )
```

```python
import functools

import jax
import jax.numpy as jnp
from jax import lax
from jax.experimental import pallas as pl
from jax.experimental.pallas import tpu as pltpu
from jax.sharding import PartitionSpec as P


HMAX = 12
ROUNDS = 2
CORE = 1
AXIS_X = 2
AXIS_Y = 4


def padded_2(cells, sides, width):
    for axis, dim in sides:
        count = lax.axis_size(axis)
        ends = count - 1
        head = lax.slice_in_dim(cells, 0, width, axis=dim)
        tail = lax.slice_in_dim(cells, cells.shape[dim] - width, cells.shape[dim], axis=dim)
        cells = jnp.concatenate(
            [
                lax.ppermute(tail, axis, [(i, (i + 1) % count) for i in range(ends)]),
                cells,
                lax.ppermute(head, axis, [((i + 1) % count, i) for i in range(ends)]),
            ],
            axis=dim,
        )
    return cells


def pair_block(own, other, windows):
    turned = jnp.concatenate([-other[:, :, windows:], other[:, :, :windows]], axis=2)
    right = jnp.concatenate([other, turned], axis=1)
    product = jnp.einsum("fcw,fdw->fcd", own, right, preferred_element_type=jnp.float32)
    return (product * (1.0 / windows)).astype(jnp.bfloat16)


def whitening_scale(spectra, half_width):
    bins, chans, columns = spectra.shape
    windows = columns // 2
    raw = spectra.astype(jnp.float32)
    power = jnp.sum(raw * raw, axis=2)
    padded = padded_2(power, (("band", 0),), HMAX)
    first = lax.axis_index("band") * bins - HMAX
    position = first + jnp.arange(bins + 2 * HMAX, dtype=jnp.int32)
    present = ((position >= 0) & (position < bins * lax.axis_size("band"))).astype(jnp.float32)[
        :, None
    ]
    total = jnp.zeros((bins, chans), jnp.float32)
    count = jnp.zeros((bins, chans), jnp.float32)
    for offset in range(-HMAX, HMAX + 1):
        inside = (abs(offset) <= half_width).astype(jnp.float32)[None, :]
        total = total + padded[HMAX + offset : HMAX + offset + bins] * inside
        count = count + present[HMAX + offset : HMAX + offset + bins] * inside
    return lax.rsqrt(total / (2.0 * windows * count) + 1e-06)


def whitened(raw, scale):
    return (raw.astype(jnp.float32) * scale[..., None]).astype(jnp.bfloat16)


def general_body(spectra, half_width, partner):
    bins, chans, columns = spectra.shape
    windows = columns // 2
    white = whitened(spectra, whitening_scale(spectra, half_width))
    blocks = lax.axis_size("chan")
    piece = chans // blocks
    sectioned = white.reshape(bins, blocks, piece, columns)
    results = [pair_block(white, white, windows)]
    for step in range(ROUNDS):
        held = lax.all_to_all(sectioned, "chan", split_axis=1, concat_axis=1, tiled=True)
        chosen = jnp.take(held, partner[step], axis=1)
        other = lax.all_to_all(chosen, "chan", split_axis=1, concat_axis=1, tiled=True)
        results.append(pair_block(white, other.reshape(bins, chans, columns), windows))
    return jnp.stack(results)


MIB = 1 << 20


def swap(values, offset):
    return lax.ppermute(values, "chan", [(i, i ^ offset) for i in range(lax.axis_size("chan"))])


SIDES = ((AXIS_X, AXIS_Y), (AXIS_Y, AXIS_X))
NEEDS, OFFSETS, HALF, LISTS = 0, 2, 4, 8
SEND, TAKE, THEIRS, LIST = 0, 4, 6, 8


def line_of(first):
    return (0, CORE, first, first | CORE)


def route_kernel(devices, device_ref, partner_ref, out_ref):
    def needed(sender, first, second):
        receiver = sender ^ second
        wanted = [
            partner_ref[r, who] for r in range(ROUNDS) for who in (receiver, receiver ^ CORE)
        ]
        need = []
        for place in line_of(first):
            hit = (sender ^ wanted[0]) == place
            for want in wanted[1:]:
                hit = hit | ((sender ^ want) == place)
            need.append(hit.astype(jnp.int32))
        return need

    def slots(need):
        slot = [jnp.int32(0)]
        for flag in need[:-1]:
            slot.append(slot[-1] + flag)
        return slot

    device = device_ref[0]
    for place in range(LISTS + 2 * LIST):
        out_ref[place] = 0
    for r in range(ROUNDS):
        out_ref[OFFSETS + r] = device ^ partner_ref[r, device]
    out_ref[HALF] = device & CORE
    for side, (first, second) in enumerate(SIDES):
        most = jnp.int32(0)
        for chip in range(0, devices, 2):
            need = needed(jnp.int32(chip), first, second)
            most = jnp.maximum(most, need[0] + need[1] + need[2] + need[3])
        out_ref[NEEDS + side] = most
        base = LISTS + side * LIST
        need = needed(device, first, second)
        slot = slots(need)
        for s in range(4):
            value = jnp.int32(0)
            for place in range(4):
                value = value + place * need[place] * (slot[place] == s).astype(jnp.int32)
            out_ref[base + SEND + s] = value
        mine = slots(needed(device ^ second, first, second))
        theirs = slots(needed(device ^ CORE ^ second, first, second))
        for r in range(ROUNDS):
            offset = device ^ partner_ref[r, device]
            take, other = jnp.int32(0), jnp.int32(0)
            for place, bits in enumerate(line_of(first)):
                near = (offset == bits).astype(jnp.int32) * place
                take += near + (offset == (bits | second)).astype(jnp.int32) * (4 + mine[place])
                other += near + (offset == ((bits ^ CORE) | second)).astype(jnp.int32) * (
                    4 + theirs[place]
                )
            out_ref[base + TAKE + r] = take
            out_ref[base + THEIRS + r] = other


def routes(device, partner):
    smem = pl.BlockSpec(memory_space=pltpu.SMEM)
    return pl.pallas_call(
        functools.partial(route_kernel, partner.shape[1]),
        out_shape=jax.ShapeDtypeStruct((LISTS + 2 * LIST,), jnp.int32),
        in_specs=[smem, smem],
        out_specs=smem,
        name="route",
    )(device.reshape(1), partner)


def column(row):
    return jnp.transpose(jnp.broadcast_to(row, (8, row.shape[1])))[:, :1]


def multiply(both, other, out_ref, at, bin_at):
    chans, columns = other.shape
    product = lax.dot_general(
        both, other, (((1,), (1,)), ((), ())), preferred_element_type=jnp.float32
    )
    product = (product * (1.0 / (columns // 2))).astype(jnp.bfloat16)
    out_ref[at, bin_at, :, :chans] = product[:chans]
    out_ref[at, bin_at, :, chans:] = product[chans:]


def own_kernel(raw, scale, both_ref, out_ref):
    step, chans, columns = raw.shape
    first = pl.program_id(0) * step

    for b in range(step):
        white = raw[b].astype(jnp.float32) * column(scale[pl.ds(first + b, 1), :])
        lane = lax.broadcasted_iota(jnp.int32, (chans, columns), 1)
        turned = pltpu.roll(jnp.where(lane < columns // 2, -white, white), columns // 2, 1)
        white, turned = white.astype(jnp.bfloat16), turned.astype(jnp.bfloat16)
        both_ref[b, :chans] = white
        both_ref[b, chans:] = turned
        multiply(jnp.concatenate([white, turned]), white, out_ref, 0, b)


def own_products(spectra, scale):
    bins, chans, columns = spectra.shape
    step = 3
    return pl.pallas_call(
        own_kernel,
        out_shape=(
            jax.ShapeDtypeStruct((bins, 2 * chans, columns), jnp.bfloat16),
            jax.ShapeDtypeStruct((1 + ROUNDS, bins, chans, 2 * chans), jnp.bfloat16),
        ),
        grid=(bins // step,),
        in_specs=[
            pl.BlockSpec((step, chans, columns), lambda i: (i, 0, 0)),
            pl.BlockSpec((bins, chans), lambda i: (0, 0)),
        ],
        out_specs=[
            pl.BlockSpec((step, 2 * chans, columns), lambda i: (i, 0, 0)),
            pl.BlockSpec((1, step, chans, 2 * chans), lambda i: (0, i, 0, 0)),
        ],
        cost_estimate=pl.CostEstimate(
            flops=4 * bins * chans * chans * columns,
            bytes_accessed=2 * bins * chans * (3 * columns + 2 * chans),
            transcendentals=0,
        ),
        compiler_params=pltpu.CompilerParams(vmem_limit_bytes=16 * MIB),
        name="own_products",
    )(spectra, scale)


def send_kernel(side, start, route, own, sister, near, far, out_ref, held, arrived, left):
    slots, part = held.shape[:2]
    base = LISTS + side * LIST + SEND
    at = route[HALF] * part
    sources = (
        own.at[pl.ds(start + at, part)],
        sister.at[pl.ds(start + at, part)],
        near.at[pl.ds(at, part)],
        far.at[pl.ds(at, part)],
    )
    for s in range(slots):
        for place, source in enumerate(sources):

            @pl.when(route[base + s] == place)
            def _():
                pltpu.make_async_copy(source, held.at[s], arrived.at[s]).start()

    for s in range(slots):
        pltpu.make_async_copy(sources[0], held.at[s], arrived.at[s]).wait()
        pltpu.make_async_copy(held.at[s], out_ref.at[s], left.at[s]).start()
    for s in range(slots):
        pltpu.make_async_copy(held.at[s], out_ref.at[s], left.at[s]).wait()


def sends(side, slots, start, part, route, own, sister, near, far):
    chans, columns = own.shape[1:]
    anywhere = pl.BlockSpec(memory_space=pl.ANY)
    smem = pl.BlockSpec(memory_space=pltpu.SMEM)
    return pl.pallas_call(
        functools.partial(send_kernel, side, start),
        out_shape=jax.ShapeDtypeStruct((slots, part, chans, columns), jnp.bfloat16),
        in_specs=[smem] + [anywhere] * 4,
        out_specs=anywhere,
        scratch_shapes=[
            pltpu.VMEM((slots, part, chans, columns), jnp.bfloat16),
            pltpu.SemaphoreType.DMA((slots,)),
            pltpu.SemaphoreType.DMA((slots,)),
        ],
        cost_estimate=pl.CostEstimate(
            flops=0, bytes_accessed=4 * slots * part * chans * columns, transcendentals=0
        ),
        compiler_params=pltpu.CompilerParams(vmem_limit_bytes=6 * MIB),
        name="send",
    )(route, own, sister, near, far)


def pair_kernel(parts, offset, which, raw, inside, unroll, route, both, sister, *refs):
    out_ref, held, done, done_out, owned, scale, owned_in, held_in, scale_in = refs[-9:]
    if raw:
        scales, refs = refs[0], refs[1:]
    half = route[HALF] if which == TAKE else 1 - route[HALF]
    total = sum(parts)
    sides = []
    for side, part in enumerate(parts):
        if part:
            sides.append((side, part, *refs[:3]))
            refs = refs[3:]

    def place_of(side, r):
        return route[LISTS + side * LIST + which + r]

    def bin_of(j):
        return jnp.where(j < parts[0], half * parts[0] + j, parts[0] + half * parts[1] + j)

    if raw:
        for r in range(ROUNDS):
            source = scales.at[route[OFFSETS + r]]
            pltpu.make_async_copy(source, scale.at[r], scale_in.at[r]).start()
    if not inside:
        for side, part, near, far, got in sides:
            for local in range(part):
                j = local + (parts[0] if side else 0)
                at = half * part + local
                start = 2 * parts[0] if side else 0
                pltpu.make_async_copy(both.at[offset + start + at], owned.at[j], owned_in.at[j]).start()
                for r in range(ROUNDS):
                    place = place_of(side, r)
                    for chosen, source in (
                        (place <= 1, sister.at[start + at]),
                        (place == 2, near.at[at]),
                        (place == 3, far.at[at]),
                    ):

                        @pl.when(chosen)
                        def _():
                            pltpu.make_async_copy(source, held.at[r, j], held_in.at[r, j]).start()

    if raw:
        for r in range(ROUNDS):
            pltpu.make_async_copy(scales.at[0], scale.at[r], scale_in.at[r]).wait()

    def ready(j):
        for side, part, near, far, got in sides:

            @pl.when((j >= parts[0]) == (side == 1))
            def _():
                local = j - (parts[0] if side else 0)
                at = half * part + local
                for r in range(ROUNDS):
                    place = place_of(side, r)

                    @pl.when(place >= 4)
                    def _():
                        held[r, j] = got[place - 4, local]

                    if inside:
                        for chosen, source, where in (
                            (place <= 1, sister, bin_of(j)),
                            (place == 2, near, at),
                            (place == 3, far, at),
                        ):

                            @pl.when(chosen)
                            def _():
                                held[r, j] = source[where]

                    else:

                        @pl.when(place < 4)
                        def _():
                            pltpu.make_async_copy(
                                sister.at[0], held.at[r, j], held_in.at[r, j]
                            ).wait()

        if not inside:
            pltpu.make_async_copy(both.at[0], owned.at[j], owned_in.at[j]).wait()

    def compute(j):
        own = both[bin_of(j)] if inside else owned[j]
        for r in range(ROUNDS):
            other = held[r, j]
            if raw:
                rows = column(scale[r, pl.ds(offset + bin_of(j), 1), :])
                other = (other.astype(jnp.float32) * rows).astype(jnp.bfloat16)
            multiply(own, other, done, j, r)

    def leave(j):
        target = out_ref.at[pl.ds(1, ROUNDS), offset + bin_of(j)]
        return pltpu.make_async_copy(done.at[j], target, done_out.at[j])

    def step(i, carry):
        for k in range(unroll):
            ready(i * unroll + k)
        for k in range(unroll):
            compute(i * unroll + k)
            leave(i * unroll + k).start()
        return carry

    lax.fori_loop(0, total // unroll, step, 0)
    for j in range(total):
        leave(j).wait()


def pair_products(
    which, parts, offset, inside, unroll, route, both, sister, scales, pieces, result
):
    chans, columns = sister.shape[1:]
    anywhere = pl.BlockSpec(memory_space=pl.ANY)
    within = pl.BlockSpec(memory_space=pltpu.VMEM)
    place = within if inside else anywhere
    raw = scales is not None
    operands = [route, both, sister]
    in_specs = [pl.BlockSpec(memory_space=pltpu.SMEM), place, place]
    if raw:
        operands.append(scales)
        in_specs.append(anywhere)
    for piece in pieces:
        operands += list(piece)
        in_specs += [place, place, within]
    total = sum(parts)
    fetched = 1 if inside else total
    bins = scales.shape[1] if raw else 8
    return pl.pallas_call(
        lambda *refs: pair_kernel(
            parts, offset, which, raw, inside, unroll, *refs[: len(operands)], *refs[len(operands) + 1 :]
        ),
        out_shape=jax.ShapeDtypeStruct(result.shape, result.dtype),
        in_specs=in_specs + [anywhere],
        out_specs=anywhere,
        scratch_shapes=[
            pltpu.VMEM((ROUNDS, total, chans, columns), jnp.bfloat16),
            pltpu.VMEM((total, ROUNDS, chans, 2 * chans), jnp.bfloat16),
            pltpu.SemaphoreType.DMA((total,)),
            pltpu.VMEM((fetched, 2 * chans, columns), jnp.bfloat16),
            pltpu.VMEM((ROUNDS, bins, chans), jnp.float32),
            pltpu.SemaphoreType.DMA((total,)),
            pltpu.SemaphoreType.DMA((ROUNDS, total)),
            pltpu.SemaphoreType.DMA((ROUNDS,)),
        ],
        input_output_aliases={len(operands): 0},
        cost_estimate=pl.CostEstimate(
            flops=8 * total * chans * chans * columns,
            bytes_accessed=8 * total * chans * (columns + chans),
            transcendentals=0,
        ),
        compiler_params=pltpu.CompilerParams(vmem_limit_bytes=(16 if inside else 30) * MIB),
    )(*operands, result)


def exchange(slots, pairs, spectra, half_width, route):
    ends = [0]
    for parts in pairs:
        ends.append(ends[-1] + 2 * sum(parts))

    def piece_of(values, p, side):
        start = 2 * pairs[p][0] if side else 0
        return values[start : start + 2 * pairs[p][side]]

    def near_of(values, p):
        near = [None, None]
        for side, (first, second) in enumerate(SIDES):
            if pairs[p][side]:
                near[side] = swap(piece_of(values, p, side), first)
        return near

    near = [near_of(spectra, 0)]
    owns = [spectra]
    sisters = [swap(owns[0], CORE)]
    scale = whitening_scale(spectra, half_width)
    for p in range(1, len(pairs)):
        owns.append(whitened(spectra[ends[p] : ends[p + 1]], scale[ends[p] : ends[p + 1]]))
        near.append(near_of(owns[p], p))
        sisters.append(swap(owns[p], CORE))
    couple = jnp.stack([scale, swap(scale, CORE)])
    scales = [couple]
    for offset in (AXIS_X, AXIS_Y, AXIS_X | AXIS_Y):
        scales.append(swap(couple, offset))
    scales = jnp.concatenate(scales)
    both, result = own_products(spectra, scale)
    far, got = [], []
    for p, parts in enumerate(pairs):
        far.append([None, None])
        got.append([None, None])
        for side, (first, second) in enumerate(SIDES):
            part = parts[side]
            if part:
                far[p][side] = swap(near[p][side], CORE)
                sent = sends(
                    side,
                    slots,
                    2 * parts[0] if side else 0,
                    part,
                    route,
                    owns[p],
                    sisters[p],
                    near[p][side],
                    far[p][side],
                )
                got[p][side] = swap(sent, second)
    for p, parts in enumerate(pairs):
        used = [side for side in (0, 1) if parts[side]]
        shared = {}
        for side in used:
            shared[side] = swap(got[p][side], CORE)
        owned = both[ends[p] : ends[p + 1]] if p else both
        for which, table in ((TAKE, {side: got[p][side] for side in used}), (THEIRS, shared)):
            pieces = [(near[p][side], far[p][side], table[side]) for side in used]
            result = pair_products(
                which,
                parts,
                ends[p],
                p > 0,
                UNROLL[p],
                route,
                owned,
                sisters[p],
                None if p else scales,
                pieces,
                result,
            )
    return result


PAIRS = ((4, 4), (2, 2))
UNROLL = (1, 1)
CASES = [(2, PAIRS), (3, PAIRS), (4, PAIRS)]


def paired_body(spectra, half_width, partner):
    device = lax.axis_index("chan").astype(jnp.int32)
    route = routes(device, partner)
    most = jnp.maximum(route[NEEDS], route[NEEDS + 1])
    choices = [functools.partial(exchange, slots, pairs) for slots, pairs in CASES]
    return lax.switch(jnp.clip(most - 2, 0, 2), choices, spectra, half_width, route)


def solution(mesh):
    placed = (P("band", "chan", None), P("chan"), P())
    paired = mesh.shape["chan"] == 8
    return jax.shard_map(
        paired_body if paired else general_body,
        mesh=mesh,
        in_specs=placed,
        out_specs=P(None, "band", "chan", None),
        check_vma=False,
    )
```

```python
import functools

import jax
import jax.numpy as jnp
from jax import lax
from jax.experimental import pallas as pl
from jax.experimental.pallas import tpu as pltpu
from jax.sharding import PartitionSpec as P


HMAX = 12
ROUNDS = 2
CORE = 1
AXIS_X = 2
AXIS_Y = 4


def padded_2(cells, sides, width):
    for axis, dim in sides:
        count = lax.axis_size(axis)
        ends = count - 1
        head = lax.slice_in_dim(cells, 0, width, axis=dim)
        tail = lax.slice_in_dim(cells, cells.shape[dim] - width, cells.shape[dim], axis=dim)
        cells = jnp.concatenate(
            [
                lax.ppermute(tail, axis, [(i, (i + 1) % count) for i in range(ends)]),
                cells,
                lax.ppermute(head, axis, [((i + 1) % count, i) for i in range(ends)]),
            ],
            axis=dim,
        )
    return cells


def pair_block(own, other, windows):
    turned = jnp.concatenate([-other[:, :, windows:], other[:, :, :windows]], axis=2)
    right = jnp.concatenate([other, turned], axis=1)
    product = jnp.einsum("fcw,fdw->fcd", own, right, preferred_element_type=jnp.float32)
    return (product * (1.0 / windows)).astype(jnp.bfloat16)


def whitening_scale(spectra, half_width):
    bins, chans, columns = spectra.shape
    windows = columns // 2
    raw = spectra.astype(jnp.float32)
    power = jnp.sum(raw * raw, axis=2)
    padded = padded_2(power, (("band", 0),), HMAX)
    first = lax.axis_index("band") * bins - HMAX
    position = first + jnp.arange(bins + 2 * HMAX, dtype=jnp.int32)
    present = ((position >= 0) & (position < bins * lax.axis_size("band"))).astype(jnp.float32)[
        :, None
    ]
    total = jnp.zeros((bins, chans), jnp.float32)
    count = jnp.zeros((bins, chans), jnp.float32)
    for offset in range(-HMAX, HMAX + 1):
        inside = (abs(offset) <= half_width).astype(jnp.float32)[None, :]
        total = total + padded[HMAX + offset : HMAX + offset + bins] * inside
        count = count + present[HMAX + offset : HMAX + offset + bins] * inside
    return lax.rsqrt(total / (2.0 * windows * count) + 1e-06)


def whitened(raw, scale):
    return (raw.astype(jnp.float32) * scale[..., None]).astype(jnp.bfloat16)


def general_body(spectra, half_width, partner):
    bins, chans, columns = spectra.shape
    windows = columns // 2
    white = whitened(spectra, whitening_scale(spectra, half_width))
    blocks = lax.axis_size("chan")
    piece = chans // blocks
    sectioned = white.reshape(bins, blocks, piece, columns)
    results = [pair_block(white, white, windows)]
    for step in range(ROUNDS):
        held = lax.all_to_all(sectioned, "chan", split_axis=1, concat_axis=1, tiled=True)
        chosen = jnp.take(held, partner[step], axis=1)
        other = lax.all_to_all(chosen, "chan", split_axis=1, concat_axis=1, tiled=True)
        results.append(pair_block(white, other.reshape(bins, chans, columns), windows))
    return jnp.stack(results)


MIB = 1 << 20


def swap(values, offset):
    return lax.ppermute(values, "chan", [(i, i ^ offset) for i in range(lax.axis_size("chan"))])


SIDES = ((AXIS_X, AXIS_Y), (AXIS_Y, AXIS_X))
OFFSETS, HALF, LISTS = 0, 2, 8
SEND, TAKE, THEIRS, LIST = 0, 4, 6, 8


def line_of(first):
    return (0, CORE, first, first | CORE)


def route_kernel(devices, device_ref, partner_ref, out_ref, case_ref):
    def needed(sender, first, second):
        receiver = sender ^ second
        wanted = [
            partner_ref[r, who] for r in range(ROUNDS) for who in (receiver, receiver ^ CORE)
        ]
        need = []
        for place in line_of(first):
            hit = (sender ^ wanted[0]) == place
            for want in wanted[1:]:
                hit = hit | ((sender ^ want) == place)
            need.append(hit.astype(jnp.int32))
        return need

    def slots(need):
        slot = [jnp.int32(0)]
        for flag in need[:-1]:
            slot.append(slot[-1] + flag)
        return slot

    device = device_ref[0]
    for place in range(LISTS + 2 * LIST):
        out_ref[place] = 0
    for r in range(ROUNDS):
        out_ref[OFFSETS + r] = device ^ partner_ref[r, device]
    out_ref[HALF] = device & CORE
    most = jnp.int32(0)
    for side, (first, second) in enumerate(SIDES):
        for chip in range(0, devices, 2):
            need = needed(jnp.int32(chip), first, second)
            most = jnp.maximum(most, need[0] + need[1] + need[2] + need[3])
        base = LISTS + side * LIST
        need = needed(device, first, second)
        slot = slots(need)
        for s in range(4):
            value = jnp.int32(0)
            for place in range(4):
                value = value + place * need[place] * (slot[place] == s).astype(jnp.int32)
            out_ref[base + SEND + s] = value
        mine = slots(needed(device ^ second, first, second))
        theirs = slots(needed(device ^ CORE ^ second, first, second))
        for r in range(ROUNDS):
            offset = device ^ partner_ref[r, device]
            take, other = jnp.int32(0), jnp.int32(0)
            for place, bits in enumerate(line_of(first)):
                near = (offset == bits).astype(jnp.int32) * place
                take += near + (offset == (bits | second)).astype(jnp.int32) * (4 + mine[place])
                other += near + (offset == ((bits ^ CORE) | second)).astype(jnp.int32) * (
                    4 + theirs[place]
                )
            out_ref[base + TAKE + r] = take
            out_ref[base + THEIRS + r] = other
    case_ref[0] = jnp.clip(most - 2, 0, 2)


def column(row):
    return jnp.transpose(jnp.broadcast_to(row, (8, row.shape[1])))[:, :1]


def multiply(both, other, out_ref, at, bin_at):
    chans, columns = other.shape
    product = lax.dot_general(
        both, other, (((1,), (1,)), ((), ())), preferred_element_type=jnp.float32
    )
    product = (product * (1.0 / (columns // 2))).astype(jnp.bfloat16)
    out_ref[at, bin_at, :, :chans] = product[:chans]
    out_ref[at, bin_at, :, chans:] = product[chans:]


def own_kernel(raw, scale, both_ref, out_ref):
    step, chans, columns = raw.shape
    first = pl.program_id(0) * step

    for b in range(step):
        white = raw[b].astype(jnp.float32) * column(scale[pl.ds(first + b, 1), :])
        lane = lax.broadcasted_iota(jnp.int32, (chans, columns), 1)
        turned = pltpu.roll(jnp.where(lane < columns // 2, -white, white), columns // 2, 1)
        white, turned = white.astype(jnp.bfloat16), turned.astype(jnp.bfloat16)
        both_ref[b, :chans] = white
        both_ref[b, chans:] = turned
        multiply(jnp.concatenate([white, turned]), white, out_ref, 0, b)


def own_products(spectra, scale):
    bins, chans, columns = spectra.shape
    step = 3
    return pl.pallas_call(
        own_kernel,
        out_shape=(
            jax.ShapeDtypeStruct((bins, 2 * chans, columns), jnp.bfloat16),
            jax.ShapeDtypeStruct((1 + ROUNDS, bins, chans, 2 * chans), jnp.bfloat16),
        ),
        grid=(bins // step,),
        in_specs=[
            pl.BlockSpec((step, chans, columns), lambda i: (i, 0, 0)),
            pl.BlockSpec((bins, chans), lambda i: (0, 0)),
        ],
        out_specs=[
            pl.BlockSpec((step, 2 * chans, columns), lambda i: (i, 0, 0)),
            pl.BlockSpec((1, step, chans, 2 * chans), lambda i: (0, i, 0, 0)),
        ],
        cost_estimate=pl.CostEstimate(
            flops=4 * bins * chans * chans * columns,
            bytes_accessed=2 * bins * chans * (3 * columns + 2 * chans),
            transcendentals=0,
        ),
        compiler_params=pltpu.CompilerParams(vmem_limit_bytes=16 * MIB),
        name="own_products",
    )(spectra, scale)


def start_kernel(devices, chunk, device_ref, partner_ref, spectra, *refs):
    out_ref, case_ref, *outs, held, arrived, left = refs
    copies = []
    begin = 0
    for piece in outs:
        for local in range(0, piece.shape[0], chunk):
            n = len(copies)
            into = pltpu.make_async_copy(
                spectra.at[pl.ds(begin + local, chunk)], held.at[n], arrived.at[n]
            )
            onto = pltpu.make_async_copy(held.at[n], piece.at[pl.ds(local, chunk)], left.at[n])
            copies.append((into, onto))
        begin += piece.shape[0]
    for into, onto in copies:
        into.start()
    route_kernel(devices, device_ref, partner_ref, out_ref, case_ref)
    for into, onto in copies:
        into.wait()
        onto.start()
    for into, onto in copies:
        onto.wait()


def starts_of(device, partner, spectra, parts):
    chans, columns = spectra.shape[1:]
    chunk = 2
    count = 2 * sum(parts) // chunk
    anywhere = pl.BlockSpec(memory_space=pl.ANY)
    smem = pl.BlockSpec(memory_space=pltpu.SMEM)
    route, case, *pieces = pl.pallas_call(
        functools.partial(start_kernel, partner.shape[1], chunk),
        out_shape=(
            jax.ShapeDtypeStruct((LISTS + 2 * LIST,), jnp.int32),
            jax.ShapeDtypeStruct((1,), jnp.int32),
            *(jax.ShapeDtypeStruct((2 * part, chans, columns), spectra.dtype) for part in parts),
        ),
        in_specs=[smem, smem, anywhere],
        out_specs=(smem, smem) + (anywhere,) * len(parts),
        scratch_shapes=[
            pltpu.VMEM((count, chunk, chans, columns), spectra.dtype),
            pltpu.SemaphoreType.DMA((count,)),
            pltpu.SemaphoreType.DMA((count,)),
        ],
        compiler_params=pltpu.CompilerParams(vmem_limit_bytes=6 * MIB),
        name="start",
    )(device.reshape(1), partner, spectra)
    return route, case, pieces


def send_kernel(side, start, route, own, sister, near, far, out_ref, held, arrived, left):
    slots, part = held.shape[:2]
    base = LISTS + side * LIST + SEND
    at = route[HALF] * part
    sources = (
        own.at[pl.ds(start + at, part)],
        sister.at[pl.ds(start + at, part)],
        near.at[pl.ds(at, part)],
        far.at[pl.ds(at, part)],
    )
    for s in range(slots):
        for place, source in enumerate(sources):

            @pl.when(route[base + s] == place)
            def _():
                pltpu.make_async_copy(source, held.at[s], arrived.at[s]).start()

    for s in range(slots):
        pltpu.make_async_copy(sources[0], held.at[s], arrived.at[s]).wait()
        pltpu.make_async_copy(held.at[s], out_ref.at[s], left.at[s]).start()
    for s in range(slots):
        pltpu.make_async_copy(held.at[s], out_ref.at[s], left.at[s]).wait()


def sends(side, slots, start, part, route, own, sister, near, far):
    chans, columns = own.shape[1:]
    anywhere = pl.BlockSpec(memory_space=pl.ANY)
    smem = pl.BlockSpec(memory_space=pltpu.SMEM)
    return pl.pallas_call(
        functools.partial(send_kernel, side, start),
        out_shape=jax.ShapeDtypeStruct((slots, part, chans, columns), jnp.bfloat16),
        in_specs=[smem] + [anywhere] * 4,
        out_specs=anywhere,
        scratch_shapes=[
            pltpu.VMEM((slots, part, chans, columns), jnp.bfloat16),
            pltpu.SemaphoreType.DMA((slots,)),
            pltpu.SemaphoreType.DMA((slots,)),
        ],
        cost_estimate=pl.CostEstimate(
            flops=0, bytes_accessed=4 * slots * part * chans * columns, transcendentals=0
        ),
        compiler_params=pltpu.CompilerParams(vmem_limit_bytes=6 * MIB),
        name="send",
    )(route, own, sister, near, far)


def pair_kernel(parts, offset, which, raw, inside, unroll, route, both, sister, *refs):
    out_ref, held, done, done_out, owned, scale, owned_in, held_in, scale_in = refs[-9:]
    if raw:
        scales, refs = refs[0], refs[1:]
    half = route[HALF] if which == TAKE else 1 - route[HALF]
    total = sum(parts)
    sides = []
    for side, part in enumerate(parts):
        if part:
            sides.append((side, part, *refs[:3]))
            refs = refs[3:]

    def place_of(side, r):
        return route[LISTS + side * LIST + which + r]

    def bin_of(j):
        return jnp.where(j < parts[0], half * parts[0] + j, parts[0] + half * parts[1] + j)

    if raw:
        for r in range(ROUNDS):
            source = scales.at[route[OFFSETS + r]]
            pltpu.make_async_copy(source, scale.at[r], scale_in.at[r]).start()
    if not inside:
        for side, part, near, far, got in sides:
            for local in range(part):
                j = local + (parts[0] if side else 0)
                at = half * part + local
                start = 2 * parts[0] if side else 0
                pltpu.make_async_copy(both.at[offset + start + at], owned.at[j], owned_in.at[j]).start()
                for r in range(ROUNDS):
                    place = place_of(side, r)
                    for chosen, source in (
                        (place <= 1, sister.at[start + at]),
                        (place == 2, near.at[at]),
                        (place == 3, far.at[at]),
                    ):

                        @pl.when(chosen)
                        def _():
                            pltpu.make_async_copy(source, held.at[r, j], held_in.at[r, j]).start()

    if raw:
        for r in range(ROUNDS):
            pltpu.make_async_copy(scales.at[0], scale.at[r], scale_in.at[r]).wait()

    def ready(j):
        for side, part, near, far, got in sides:

            @pl.when((j >= parts[0]) == (side == 1))
            def _():
                local = j - (parts[0] if side else 0)
                at = half * part + local
                for r in range(ROUNDS):
                    place = place_of(side, r)

                    @pl.when(place >= 4)
                    def _():
                        held[r, j] = got[place - 4, local]

                    if inside:
                        for chosen, source, where in (
                            (place <= 1, sister, bin_of(j)),
                            (place == 2, near, at),
                            (place == 3, far, at),
                        ):

                            @pl.when(chosen)
                            def _():
                                held[r, j] = source[where]

                    else:

                        @pl.when(place < 4)
                        def _():
                            pltpu.make_async_copy(
                                sister.at[0], held.at[r, j], held_in.at[r, j]
                            ).wait()

        if not inside:
            pltpu.make_async_copy(both.at[0], owned.at[j], owned_in.at[j]).wait()

    def compute(j):
        own = both[bin_of(j)] if inside else owned[j]
        for r in range(ROUNDS):
            other = held[r, j]
            if raw:
                rows = column(scale[r, pl.ds(offset + bin_of(j), 1), :])
                other = (other.astype(jnp.float32) * rows).astype(jnp.bfloat16)
            multiply(own, other, done, j, r)

    def leave(j):
        target = out_ref.at[pl.ds(1, ROUNDS), offset + bin_of(j)]
        return pltpu.make_async_copy(done.at[j], target, done_out.at[j])

    def step(i, carry):
        for k in range(unroll):
            ready(i * unroll + k)
        for k in range(unroll):
            compute(i * unroll + k)
            leave(i * unroll + k).start()
        return carry

    lax.fori_loop(0, total // unroll, step, 0)
    for j in range(total):
        leave(j).wait()


def pair_products(
    which, parts, offset, inside, unroll, route, both, sister, scales, pieces, result
):
    chans, columns = sister.shape[1:]
    anywhere = pl.BlockSpec(memory_space=pl.ANY)
    within = pl.BlockSpec(memory_space=pltpu.VMEM)
    place = within if inside else anywhere
    raw = scales is not None
    operands = [route, both, sister]
    in_specs = [pl.BlockSpec(memory_space=pltpu.SMEM), place, place]
    if raw:
        operands.append(scales)
        in_specs.append(anywhere)
    for piece in pieces:
        operands += list(piece)
        in_specs += [place, place, within]
    total = sum(parts)
    fetched = 1 if inside else total
    bins = scales.shape[1] if raw else 8
    return pl.pallas_call(
        lambda *refs: pair_kernel(
            parts, offset, which, raw, inside, unroll, *refs[: len(operands)], *refs[len(operands) + 1 :]
        ),
        out_shape=jax.ShapeDtypeStruct(result.shape, result.dtype),
        in_specs=in_specs + [anywhere],
        out_specs=anywhere,
        scratch_shapes=[
            pltpu.VMEM((ROUNDS, total, chans, columns), jnp.bfloat16),
            pltpu.VMEM((total, ROUNDS, chans, 2 * chans), jnp.bfloat16),
            pltpu.SemaphoreType.DMA((total,)),
            pltpu.VMEM((fetched, 2 * chans, columns), jnp.bfloat16),
            pltpu.VMEM((ROUNDS, bins, chans), jnp.float32),
            pltpu.SemaphoreType.DMA((total,)),
            pltpu.SemaphoreType.DMA((ROUNDS, total)),
            pltpu.SemaphoreType.DMA((ROUNDS,)),
        ],
        input_output_aliases={len(operands): 0},
        cost_estimate=pl.CostEstimate(
            flops=8 * total * chans * chans * columns,
            bytes_accessed=8 * total * chans * (columns + chans),
            transcendentals=0,
        ),
        compiler_params=pltpu.CompilerParams(vmem_limit_bytes=(16 if inside else 20) * MIB),
    )(*operands, result)


def exchange(slots, pairs, spectra, half_width, route, *pieces):
    ends = [0]
    for parts in pairs:
        ends.append(ends[-1] + 2 * sum(parts))

    def piece_of(values, p, side):
        start = 2 * pairs[p][0] if side else 0
        return values[start : start + 2 * pairs[p][side]]

    def near_of(pieces, p):
        near = [None, None]
        for side, (first, second) in enumerate(SIDES):
            if pairs[p][side]:
                near[side] = swap(pieces[side], first)
        return near

    near = [near_of(pieces, 0)]
    owns = [spectra]
    sisters = [swap(owns[0], CORE)]
    scale = whitening_scale(spectra, half_width)
    for p in range(1, len(pairs)):
        owns.append(whitened(spectra[ends[p] : ends[p + 1]], scale[ends[p] : ends[p + 1]]))
        near.append(near_of([piece_of(owns[p], p, side) for side in (0, 1)], p))
        sisters.append(swap(owns[p], CORE))
    couple = jnp.stack([scale, swap(scale, CORE)])
    scales = [couple]
    for offset in (AXIS_X, AXIS_Y, AXIS_X | AXIS_Y):
        scales.append(swap(couple, offset))
    scales = jnp.concatenate(scales)
    both, result = own_products(spectra, scale)
    far, got = [], []
    for p, parts in enumerate(pairs):
        far.append([None, None])
        got.append([None, None])
        for side, (first, second) in enumerate(SIDES):
            part = parts[side]
            if part:
                far[p][side] = swap(near[p][side], CORE)
                sent = sends(
                    side,
                    slots,
                    2 * parts[0] if side else 0,
                    part,
                    route,
                    owns[p],
                    sisters[p],
                    near[p][side],
                    far[p][side],
                )
                got[p][side] = swap(sent, second)
    for p, parts in enumerate(pairs):
        used = [side for side in (0, 1) if parts[side]]
        shared = {}
        for side in used:
            shared[side] = swap(got[p][side], CORE)
        owned = both[ends[p] : ends[p + 1]] if p else both
        for which, table in ((TAKE, {side: got[p][side] for side in used}), (THEIRS, shared)):
            pieces = [(near[p][side], far[p][side], table[side]) for side in used]
            result = pair_products(
                which,
                parts,
                ends[p],
                p > 0,
                UNROLL[p],
                route,
                owned,
                sisters[p],
                None if p else scales,
                pieces,
                result,
            )
    return result


PAIRS = ((4, 4), (2, 2))
UNROLL = (1, 2)
CASES = [(2, PAIRS), (3, PAIRS), (4, PAIRS)]


def paired_body(spectra, half_width, partner):
    device = lax.axis_index("chan").astype(jnp.int32)
    route, case, pieces = starts_of(device, partner, spectra, PAIRS[0])
    choices = [functools.partial(exchange, slots, pairs) for slots, pairs in CASES]
    return lax.switch(case.reshape(()), choices, spectra, half_width, route, *pieces)


def solution(mesh):
    placed = (P("band", "chan", None), P("chan"), P())
    paired = mesh.shape["chan"] == 8
    return jax.shard_map(
        paired_body if paired else general_body,
        mesh=mesh,
        in_specs=placed,
        out_specs=P(None, "band", "chan", None),
        check_vma=False,
    )
```

```python
import functools

import jax
import jax.numpy as jnp
from jax import lax
from jax.experimental import pallas as pl
from jax.experimental.pallas import tpu as pltpu
from jax.sharding import PartitionSpec as P


HMAX = 12
ROUNDS = 2
CORE = 1
AXIS_X = 2
AXIS_Y = 4


def padded_2(cells, sides, width):
    for axis, dim in sides:
        count = lax.axis_size(axis)
        ends = count - 1
        head = lax.slice_in_dim(cells, 0, width, axis=dim)
        tail = lax.slice_in_dim(cells, cells.shape[dim] - width, cells.shape[dim], axis=dim)
        cells = jnp.concatenate(
            [
                lax.ppermute(tail, axis, [(i, (i + 1) % count) for i in range(ends)]),
                cells,
                lax.ppermute(head, axis, [((i + 1) % count, i) for i in range(ends)]),
            ],
            axis=dim,
        )
    return cells


def pair_block(own, other, windows):
    turned = jnp.concatenate([-other[:, :, windows:], other[:, :, :windows]], axis=2)
    right = jnp.concatenate([other, turned], axis=1)
    product = jnp.einsum("fcw,fdw->fcd", own, right, preferred_element_type=jnp.float32)
    return (product * (1.0 / windows)).astype(jnp.bfloat16)


def whitening_scale(spectra, half_width):
    bins, chans, columns = spectra.shape
    windows = columns // 2
    raw = spectra.astype(jnp.float32)
    power = jnp.sum(raw * raw, axis=2)
    padded = padded_2(power, (("band", 0),), HMAX)
    first = lax.axis_index("band") * bins - HMAX
    position = first + jnp.arange(bins + 2 * HMAX, dtype=jnp.int32)
    present = ((position >= 0) & (position < bins * lax.axis_size("band"))).astype(jnp.float32)[
        :, None
    ]
    total = jnp.zeros((bins, chans), jnp.float32)
    count = jnp.zeros((bins, chans), jnp.float32)
    for offset in range(-HMAX, HMAX + 1):
        inside = (abs(offset) <= half_width).astype(jnp.float32)[None, :]
        total = total + padded[HMAX + offset : HMAX + offset + bins] * inside
        count = count + present[HMAX + offset : HMAX + offset + bins] * inside
    return lax.rsqrt(total / (2.0 * windows * count) + 1e-06)


def whitened(raw, scale):
    return (raw.astype(jnp.float32) * scale[..., None]).astype(jnp.bfloat16)


def general_body(spectra, half_width, partner):
    bins, chans, columns = spectra.shape
    windows = columns // 2
    white = whitened(spectra, whitening_scale(spectra, half_width))
    blocks = lax.axis_size("chan")
    piece = chans // blocks
    sectioned = white.reshape(bins, blocks, piece, columns)
    results = [pair_block(white, white, windows)]
    for step in range(ROUNDS):
        held = lax.all_to_all(sectioned, "chan", split_axis=1, concat_axis=1, tiled=True)
        chosen = jnp.take(held, partner[step], axis=1)
        other = lax.all_to_all(chosen, "chan", split_axis=1, concat_axis=1, tiled=True)
        results.append(pair_block(white, other.reshape(bins, chans, columns), windows))
    return jnp.stack(results)


MIB = 1 << 20


def swap(values, offset):
    return lax.ppermute(values, "chan", [(i, i ^ offset) for i in range(lax.axis_size("chan"))])


SIDES = ((AXIS_X, AXIS_Y), (AXIS_Y, AXIS_X))
OFFSETS, HALF, LISTS = 0, 2, 8
SEND, TAKE, THEIRS, LIST = 0, 4, 6, 8


def line_of(first):
    return (0, CORE, first, first | CORE)


def route_kernel(devices, device_ref, partner_ref, out_ref, case_ref):
    def needed(sender, first, second):
        receiver = sender ^ second
        wanted = [
            partner_ref[r, who] for r in range(ROUNDS) for who in (receiver, receiver ^ CORE)
        ]
        need = []
        for place in line_of(first):
            hit = (sender ^ wanted[0]) == place
            for want in wanted[1:]:
                hit = hit | ((sender ^ want) == place)
            need.append(hit.astype(jnp.int32))
        return need

    def slots(need):
        slot = [jnp.int32(0)]
        for flag in need[:-1]:
            slot.append(slot[-1] + flag)
        return slot

    device = device_ref[0]
    for place in range(LISTS + 2 * LIST):
        out_ref[place] = 0
    for r in range(ROUNDS):
        out_ref[OFFSETS + r] = device ^ partner_ref[r, device]
    out_ref[HALF] = device & CORE
    most = jnp.int32(0)
    for side, (first, second) in enumerate(SIDES):
        for chip in range(0, devices, 2):
            need = needed(jnp.int32(chip), first, second)
            most = jnp.maximum(most, need[0] + need[1] + need[2] + need[3])
        base = LISTS + side * LIST
        need = needed(device, first, second)
        slot = slots(need)
        for s in range(4):
            value = jnp.int32(0)
            for place in range(4):
                value = value + place * need[place] * (slot[place] == s).astype(jnp.int32)
            out_ref[base + SEND + s] = value
        mine = slots(needed(device ^ second, first, second))
        theirs = slots(needed(device ^ CORE ^ second, first, second))
        for r in range(ROUNDS):
            offset = device ^ partner_ref[r, device]
            take, other = jnp.int32(0), jnp.int32(0)
            for place, bits in enumerate(line_of(first)):
                near = (offset == bits).astype(jnp.int32) * place
                take += near + (offset == (bits | second)).astype(jnp.int32) * (4 + mine[place])
                other += near + (offset == ((bits ^ CORE) | second)).astype(jnp.int32) * (
                    4 + theirs[place]
                )
            out_ref[base + TAKE + r] = take
            out_ref[base + THEIRS + r] = other
    case_ref[0] = jnp.clip(most - 2, 0, 2)


def column(row):
    return jnp.transpose(jnp.broadcast_to(row, (8, row.shape[1])))[:, :1]


def multiply(both, other, out_ref, at, bin_at):
    chans, columns = other.shape
    product = lax.dot_general(
        both, other, (((1,), (1,)), ((), ())), preferred_element_type=jnp.float32
    )
    product = (product * (1.0 / (columns // 2))).astype(jnp.bfloat16)
    out_ref[at, bin_at, :, :chans] = product[:chans]
    out_ref[at, bin_at, :, chans:] = product[chans:]


def own_kernel(raw, scale, both_ref, out_ref):
    step, chans, columns = raw.shape
    first = pl.program_id(0) * step

    for b in range(step):
        white = raw[b].astype(jnp.float32) * column(scale[pl.ds(first + b, 1), :])
        lane = lax.broadcasted_iota(jnp.int32, (chans, columns), 1)
        turned = pltpu.roll(jnp.where(lane < columns // 2, -white, white), columns // 2, 1)
        white, turned = white.astype(jnp.bfloat16), turned.astype(jnp.bfloat16)
        both_ref[b, :chans] = white
        both_ref[b, chans:] = turned
        multiply(jnp.concatenate([white, turned]), white, out_ref, 0, b)


def own_products(spectra, scale):
    bins, chans, columns = spectra.shape
    step = 3
    return pl.pallas_call(
        own_kernel,
        out_shape=(
            jax.ShapeDtypeStruct((bins, 2 * chans, columns), jnp.bfloat16),
            jax.ShapeDtypeStruct((1 + ROUNDS, bins, chans, 2 * chans), jnp.bfloat16),
        ),
        grid=(bins // step,),
        in_specs=[
            pl.BlockSpec((step, chans, columns), lambda i: (i, 0, 0)),
            pl.BlockSpec((bins, chans), lambda i: (0, 0)),
        ],
        out_specs=[
            pl.BlockSpec((step, 2 * chans, columns), lambda i: (i, 0, 0)),
            pl.BlockSpec((1, step, chans, 2 * chans), lambda i: (0, i, 0, 0)),
        ],
        cost_estimate=pl.CostEstimate(
            flops=4 * bins * chans * chans * columns,
            bytes_accessed=2 * bins * chans * (3 * columns + 2 * chans),
            transcendentals=0,
        ),
        compiler_params=pltpu.CompilerParams(vmem_limit_bytes=16 * MIB),
        name="own_products",
    )(spectra, scale)


def start_kernel(devices, chunk, device_ref, partner_ref, spectra, *refs):
    out_ref, case_ref, *outs, held, arrived, left = refs
    copies = []
    begin = 0
    for piece in outs:
        for local in range(0, piece.shape[0], chunk):
            n = len(copies)
            into = pltpu.make_async_copy(
                spectra.at[pl.ds(begin + local, chunk)], held.at[n], arrived.at[n]
            )
            onto = pltpu.make_async_copy(held.at[n], piece.at[pl.ds(local, chunk)], left.at[n])
            copies.append((into, onto))
        begin += piece.shape[0]
    for into, onto in copies:
        into.start()
    route_kernel(devices, device_ref, partner_ref, out_ref, case_ref)
    for into, onto in copies:
        into.wait()
        onto.start()
    for into, onto in copies:
        onto.wait()


def starts_of(device, partner, spectra, parts):
    chans, columns = spectra.shape[1:]
    chunk = 2
    count = 2 * sum(parts) // chunk
    anywhere = pl.BlockSpec(memory_space=pl.ANY)
    smem = pl.BlockSpec(memory_space=pltpu.SMEM)
    route, case, *pieces = pl.pallas_call(
        functools.partial(start_kernel, partner.shape[1], chunk),
        out_shape=(
            jax.ShapeDtypeStruct((LISTS + 2 * LIST,), jnp.int32),
            jax.ShapeDtypeStruct((1,), jnp.int32),
            *(jax.ShapeDtypeStruct((2 * part, chans, columns), spectra.dtype) for part in parts),
        ),
        in_specs=[smem, smem, anywhere],
        out_specs=(smem, smem) + (anywhere,) * len(parts),
        scratch_shapes=[
            pltpu.VMEM((count, chunk, chans, columns), spectra.dtype),
            pltpu.SemaphoreType.DMA((count,)),
            pltpu.SemaphoreType.DMA((count,)),
        ],
        compiler_params=pltpu.CompilerParams(vmem_limit_bytes=6 * MIB),
        name="start",
    )(device.reshape(1), partner, spectra)
    return route, case, pieces


def send_kernel(side, start, route, own, sister, near, far, out_ref, held, arrived, left):
    slots, part = held.shape[:2]
    base = LISTS + side * LIST + SEND
    at = route[HALF] * part
    sources = (
        own.at[pl.ds(start + at, part)],
        sister.at[pl.ds(start + at, part)],
        near.at[pl.ds(at, part)],
        far.at[pl.ds(at, part)],
    )
    for s in range(slots):
        for place, source in enumerate(sources):

            @pl.when(route[base + s] == place)
            def _():
                pltpu.make_async_copy(source, held.at[s], arrived.at[s]).start()

    for s in range(slots):
        pltpu.make_async_copy(sources[0], held.at[s], arrived.at[s]).wait()
        pltpu.make_async_copy(held.at[s], out_ref.at[s], left.at[s]).start()
    for s in range(slots):
        pltpu.make_async_copy(held.at[s], out_ref.at[s], left.at[s]).wait()


def sends(side, slots, start, part, route, own, sister, near, far):
    chans, columns = own.shape[1:]
    anywhere = pl.BlockSpec(memory_space=pl.ANY)
    smem = pl.BlockSpec(memory_space=pltpu.SMEM)
    return pl.pallas_call(
        functools.partial(send_kernel, side, start),
        out_shape=jax.ShapeDtypeStruct((slots, part, chans, columns), jnp.bfloat16),
        in_specs=[smem] + [anywhere] * 4,
        out_specs=anywhere,
        scratch_shapes=[
            pltpu.VMEM((slots, part, chans, columns), jnp.bfloat16),
            pltpu.SemaphoreType.DMA((slots,)),
            pltpu.SemaphoreType.DMA((slots,)),
        ],
        cost_estimate=pl.CostEstimate(
            flops=0, bytes_accessed=4 * slots * part * chans * columns, transcendentals=0
        ),
        compiler_params=pltpu.CompilerParams(vmem_limit_bytes=6 * MIB),
        name="send",
    )(route, own, sister, near, far)


def pair_kernel(parts, offset, which, raw, inside, unroll, route, both, sister, *refs):
    out_ref, held, done, done_out, owned, scale, pure, owned_in, held_in, scale_in = refs[-10:]
    if raw:
        scales, refs = refs[0], refs[1:]
    half = route[HALF] if which == TAKE else 1 - route[HALF]
    total = sum(parts)
    sides = []
    for side, part in enumerate(parts):
        if part:
            sides.append((side, part, *refs[:3]))
            refs = refs[3:]

    def place_of(side, r):
        return route[LISTS + side * LIST + which + r]

    def bin_of(j):
        return jnp.where(j < parts[0], half * parts[0] + j, parts[0] + half * parts[1] + j)

    if raw:
        for r in range(ROUNDS):
            source = scales.at[route[OFFSETS + r]]
            pltpu.make_async_copy(source, scale.at[r], scale_in.at[r]).start()

    def fetch(j):
        pltpu.make_async_copy(both.at[offset + bin_of(j)], owned.at[j], owned_in.at[j]).start()
        for side, part, near, far, got in sides:

            @pl.when((j >= parts[0]) == (side == 1))
            def _():
                at = half * part + j - (parts[0] if side else 0)
                for r in range(ROUNDS):
                    place = place_of(side, r)
                    for chosen, source in (
                        (place <= 1, sister.at[bin_of(j)]),
                        (place == 2, near.at[at]),
                        (place == 3, far.at[at]),
                    ):

                        @pl.when(chosen)
                        def _():
                            pltpu.make_async_copy(source, held.at[r, j], held_in.at[r, j]).start()

    if not inside:
        for j in range(AHEAD):
            fetch(jnp.int32(j))

    if raw:
        for r in range(ROUNDS):
            pltpu.make_async_copy(scales.at[0], scale.at[r], scale_in.at[r]).wait()

    def ready(j):
        for side, part, near, far, got in sides:

            @pl.when((j >= parts[0]) == (side == 1))
            def _():
                local = j - (parts[0] if side else 0)
                at = half * part + local
                for r in range(ROUNDS):
                    place = place_of(side, r)

                    @pl.when(place >= 4)
                    def _():
                        held[r, j] = got[place - 4, local]

                    if inside:
                        for chosen, source, where in (
                            (place <= 1, sister, bin_of(j)),
                            (place == 2, near, at),
                            (place == 3, far, at),
                        ):

                            @pl.when(chosen)
                            def _():
                                held[r, j] = source[where]

                    else:

                        @pl.when(place < 4)
                        def _():
                            pltpu.make_async_copy(
                                sister.at[0], held.at[r, j], held_in.at[r, j]
                            ).wait()

        if not inside:
            pltpu.make_async_copy(both.at[0], owned.at[j], owned_in.at[j]).wait()

    def compute(j):
        own = both[bin_of(j)] if inside else owned[j]
        for r in range(ROUNDS):
            other = pure[lax.rem(j, 2), r] if raw else held[r, j]
            multiply(own, other, done, j, r)

    def whiten(j):
        for r in range(ROUNDS):
            rows = column(scale[r, pl.ds(offset + bin_of(j), 1), :])
            white = held[r, j].astype(jnp.float32) * rows
            pure[lax.rem(j, 2), r] = white.astype(jnp.bfloat16)

    def leave(j):
        target = out_ref.at[pl.ds(1, ROUNDS), offset + bin_of(j)]
        return pltpu.make_async_copy(done.at[j], target, done_out.at[j])

    def step(i, carry):
        if not inside:

            @pl.when(i + AHEAD < total)
            def _():
                fetch(i + AHEAD)

        if raw:

            @pl.when(i + 1 < total)
            def _():
                ready(i + 1)

            compute(i)
            whiten(jnp.minimum(i + 1, total - 1))
            leave(i).start()
            return carry
        for k in range(unroll):
            ready(i * unroll + k)
        for k in range(unroll):
            compute(i * unroll + k)
            leave(i * unroll + k).start()
        return carry

    if raw:
        ready(jnp.int32(0))
        whiten(jnp.int32(0))
    lax.fori_loop(0, total // unroll, step, 0)
    for j in range(total):
        leave(j).wait()


def pair_products(
    which, parts, offset, inside, unroll, route, both, sister, scales, pieces, result
):
    chans, columns = sister.shape[1:]
    anywhere = pl.BlockSpec(memory_space=pl.ANY)
    within = pl.BlockSpec(memory_space=pltpu.VMEM)
    place = within if inside else anywhere
    raw = scales is not None
    operands = [route, both, sister]
    in_specs = [pl.BlockSpec(memory_space=pltpu.SMEM), place, place]
    if raw:
        operands.append(scales)
        in_specs.append(anywhere)
    for piece in pieces:
        operands += list(piece)
        in_specs += [place, place, within]
    total = sum(parts)
    fetched = 1 if inside else total
    bins = scales.shape[1] if raw else 8
    return pl.pallas_call(
        lambda *refs: pair_kernel(
            parts, offset, which, raw, inside, unroll, *refs[: len(operands)], *refs[len(operands) + 1 :]
        ),
        out_shape=jax.ShapeDtypeStruct(result.shape, result.dtype),
        in_specs=in_specs + [anywhere],
        out_specs=anywhere,
        scratch_shapes=[
            pltpu.VMEM((ROUNDS, total, chans, columns), jnp.bfloat16),
            pltpu.VMEM((total, ROUNDS, chans, 2 * chans), jnp.bfloat16),
            pltpu.SemaphoreType.DMA((total,)),
            pltpu.VMEM((fetched, 2 * chans, columns), jnp.bfloat16),
            pltpu.VMEM((ROUNDS, bins, chans), jnp.float32),
            pltpu.VMEM((2, ROUNDS, chans if raw else 8, columns), jnp.bfloat16),
            pltpu.SemaphoreType.DMA((total,)),
            pltpu.SemaphoreType.DMA((ROUNDS, total)),
            pltpu.SemaphoreType.DMA((ROUNDS,)),
        ],
        input_output_aliases={len(operands): 0},
        cost_estimate=pl.CostEstimate(
            flops=8 * total * chans * chans * columns,
            bytes_accessed=8 * total * chans * (columns + chans),
            transcendentals=0,
        ),
        compiler_params=pltpu.CompilerParams(vmem_limit_bytes=(16 if inside else 21) * MIB),
    )(*operands, result)


def exchange(slots, pairs, spectra, half_width, route, *pieces):
    ends = [0]
    for parts in pairs:
        ends.append(ends[-1] + 2 * sum(parts))

    def piece_of(values, p, side):
        start = 2 * pairs[p][0] if side else 0
        return values[start : start + 2 * pairs[p][side]]

    def near_of(pieces, p):
        near = [None, None]
        for side, (first, second) in enumerate(SIDES):
            if pairs[p][side]:
                near[side] = swap(pieces[side], first)
        return near

    near = [near_of(pieces, 0)]
    owns = [spectra]
    sisters = [swap(owns[0], CORE)]
    scale = whitening_scale(spectra, half_width)
    for p in range(1, len(pairs)):
        owns.append(whitened(spectra[ends[p] : ends[p + 1]], scale[ends[p] : ends[p + 1]]))
        near.append(near_of([piece_of(owns[p], p, side) for side in (0, 1)], p))
        sisters.append(swap(owns[p], CORE))
    couple = jnp.stack([scale, swap(scale, CORE)])
    scales = [couple]
    for offset in (AXIS_X, AXIS_Y, AXIS_X | AXIS_Y):
        scales.append(swap(couple, offset))
    scales = jnp.concatenate(scales)
    both, result = own_products(spectra, scale)
    far, got = [], []
    for p, parts in enumerate(pairs):
        far.append([None, None])
        got.append([None, None])
        for side, (first, second) in enumerate(SIDES):
            part = parts[side]
            if part:
                far[p][side] = swap(near[p][side], CORE)
                sent = sends(
                    side,
                    slots,
                    2 * parts[0] if side else 0,
                    part,
                    route,
                    owns[p],
                    sisters[p],
                    near[p][side],
                    far[p][side],
                )
                got[p][side] = swap(sent, second)
    for p, parts in enumerate(pairs):
        used = [side for side in (0, 1) if parts[side]]
        shared = {}
        for side in used:
            shared[side] = swap(got[p][side], CORE)
        owned = both[ends[p] : ends[p + 1]] if p else both
        for which, table in ((TAKE, {side: got[p][side] for side in used}), (THEIRS, shared)):
            pieces = [(near[p][side], far[p][side], table[side]) for side in used]
            result = pair_products(
                which,
                parts,
                ends[p],
                p > 0,
                UNROLL[p],
                route,
                owned,
                sisters[p],
                None if p else scales,
                pieces,
                result,
            )
    return result


PAIRS = ((4, 4), (2, 2))
UNROLL = (1, 2)
AHEAD = 3
CASES = [(2, PAIRS), (3, PAIRS), (4, PAIRS)]


def paired_body(spectra, half_width, partner):
    device = lax.axis_index("chan").astype(jnp.int32)
    route, case, pieces = starts_of(device, partner, spectra, PAIRS[0])
    choices = [functools.partial(exchange, slots, pairs) for slots, pairs in CASES]
    return lax.switch(case.reshape(()), choices, spectra, half_width, route, *pieces)


def solution(mesh):
    placed = (P("band", "chan", None), P("chan"), P())
    paired = mesh.shape["chan"] == 8
    return jax.shard_map(
        paired_body if paired else general_body,
        mesh=mesh,
        in_specs=placed,
        out_specs=P(None, "band", "chan", None),
        check_vma=False,
    )
```

```python
import functools

import jax
import jax.numpy as jnp
from jax import lax
from jax.experimental import pallas as pl
from jax.experimental.pallas import tpu as pltpu
from jax.sharding import PartitionSpec as P


HMAX = 12
ROUNDS = 2
CORE = 1
AXIS_X = 2
AXIS_Y = 4


def padded_2(cells, sides, width):
    for axis, dim in sides:
        count = lax.axis_size(axis)
        ends = count - 1
        head = lax.slice_in_dim(cells, 0, width, axis=dim)
        tail = lax.slice_in_dim(cells, cells.shape[dim] - width, cells.shape[dim], axis=dim)
        cells = jnp.concatenate(
            [
                lax.ppermute(tail, axis, [(i, (i + 1) % count) for i in range(ends)]),
                cells,
                lax.ppermute(head, axis, [((i + 1) % count, i) for i in range(ends)]),
            ],
            axis=dim,
        )
    return cells


def pair_block(own, other, windows):
    turned = jnp.concatenate([-other[:, :, windows:], other[:, :, :windows]], axis=2)
    right = jnp.concatenate([other, turned], axis=1)
    product = jnp.einsum("fcw,fdw->fcd", own, right, preferred_element_type=jnp.float32)
    return (product * (1.0 / windows)).astype(jnp.bfloat16)


def whitening_scale(spectra, half_width):
    bins, chans, columns = spectra.shape
    windows = columns // 2
    raw = spectra.astype(jnp.float32)
    power = jnp.sum(raw * raw, axis=2)
    padded = padded_2(power, (("band", 0),), HMAX)
    first = lax.axis_index("band") * bins - HMAX
    position = first + jnp.arange(bins + 2 * HMAX, dtype=jnp.int32)
    present = ((position >= 0) & (position < bins * lax.axis_size("band"))).astype(jnp.float32)[
        :, None
    ]
    total = jnp.zeros((bins, chans), jnp.float32)
    count = jnp.zeros((bins, chans), jnp.float32)
    for offset in range(-HMAX, HMAX + 1):
        inside = (abs(offset) <= half_width).astype(jnp.float32)[None, :]
        total = total + padded[HMAX + offset : HMAX + offset + bins] * inside
        count = count + present[HMAX + offset : HMAX + offset + bins] * inside
    return lax.rsqrt(total / (2.0 * windows * count) + 1e-06)


def whitened(raw, scale):
    return (raw.astype(jnp.float32) * scale[..., None]).astype(jnp.bfloat16)


def general_body(spectra, half_width, partner):
    bins, chans, columns = spectra.shape
    windows = columns // 2
    white = whitened(spectra, whitening_scale(spectra, half_width))
    blocks = lax.axis_size("chan")
    piece = chans // blocks
    sectioned = white.reshape(bins, blocks, piece, columns)
    results = [pair_block(white, white, windows)]
    for step in range(ROUNDS):
        held = lax.all_to_all(sectioned, "chan", split_axis=1, concat_axis=1, tiled=True)
        chosen = jnp.take(held, partner[step], axis=1)
        other = lax.all_to_all(chosen, "chan", split_axis=1, concat_axis=1, tiled=True)
        results.append(pair_block(white, other.reshape(bins, chans, columns), windows))
    return jnp.stack(results)


MIB = 1 << 20


def swap(values, offset):
    return lax.ppermute(values, "chan", [(i, i ^ offset) for i in range(lax.axis_size("chan"))])


SIDES = ((AXIS_X, AXIS_Y), (AXIS_Y, AXIS_X))
OFFSETS, HALF, LISTS = 0, 2, 8
SEND, TAKE, THEIRS, LIST = 0, 4, 6, 8


def line_of(first):
    return (0, CORE, first, first | CORE)


def route_kernel(devices, device_ref, partner_ref, out_ref, case_ref):
    def needed(sender, first, second):
        receiver = sender ^ second
        wanted = [
            partner_ref[r, who] for r in range(ROUNDS) for who in (receiver, receiver ^ CORE)
        ]
        need = []
        for place in line_of(first):
            hit = (sender ^ wanted[0]) == place
            for want in wanted[1:]:
                hit = hit | ((sender ^ want) == place)
            need.append(hit.astype(jnp.int32))
        return need

    def slots(need):
        slot = [jnp.int32(0)]
        for flag in need[:-1]:
            slot.append(slot[-1] + flag)
        return slot

    device = device_ref[0]
    for place in range(LISTS + 2 * LIST):
        out_ref[place] = 0
    for r in range(ROUNDS):
        out_ref[OFFSETS + r] = device ^ partner_ref[r, device]
    out_ref[HALF] = device & CORE
    most = jnp.int32(0)
    for side, (first, second) in enumerate(SIDES):
        for chip in range(0, devices, 2):
            need = needed(jnp.int32(chip), first, second)
            most = jnp.maximum(most, need[0] + need[1] + need[2] + need[3])
        base = LISTS + side * LIST
        need = needed(device, first, second)
        slot = slots(need)
        for s in range(4):
            value = jnp.int32(0)
            for place in range(4):
                value = value + place * need[place] * (slot[place] == s).astype(jnp.int32)
            out_ref[base + SEND + s] = value
        mine = slots(needed(device ^ second, first, second))
        theirs = slots(needed(device ^ CORE ^ second, first, second))
        for r in range(ROUNDS):
            offset = device ^ partner_ref[r, device]
            take, other = jnp.int32(0), jnp.int32(0)
            for place, bits in enumerate(line_of(first)):
                near = (offset == bits).astype(jnp.int32) * place
                take += near + (offset == (bits | second)).astype(jnp.int32) * (4 + mine[place])
                other += near + (offset == ((bits ^ CORE) | second)).astype(jnp.int32) * (
                    4 + theirs[place]
                )
            out_ref[base + TAKE + r] = take
            out_ref[base + THEIRS + r] = other
    case_ref[0] = jnp.clip(most - 2, 0, 2)


def column(row):
    return jnp.transpose(jnp.broadcast_to(row, (8, row.shape[1])))[:, :1]


def multiply(both, other, out_ref, at, bin_at):
    chans, columns = other.shape
    product = lax.dot_general(
        both, other, (((1,), (1,)), ((), ())), preferred_element_type=jnp.float32
    )
    product = (product * (1.0 / (columns // 2))).astype(jnp.bfloat16)
    out_ref[at, bin_at, :, :chans] = product[:chans]
    out_ref[at, bin_at, :, chans:] = product[chans:]


def own_kernel(raw, scale, both_ref, out_ref):
    step, chans, columns = raw.shape
    first = pl.program_id(0) * step

    for b in range(step):
        white = raw[b].astype(jnp.float32) * column(scale[pl.ds(first + b, 1), :])
        lane = lax.broadcasted_iota(jnp.int32, (chans, columns), 1)
        turned = pltpu.roll(jnp.where(lane < columns // 2, -white, white), columns // 2, 1)
        white, turned = white.astype(jnp.bfloat16), turned.astype(jnp.bfloat16)
        both_ref[b, :chans] = white
        both_ref[b, chans:] = turned
        multiply(jnp.concatenate([white, turned]), white, out_ref, 0, b)


def own_products(spectra, scale):
    bins, chans, columns = spectra.shape
    step = 3
    return pl.pallas_call(
        own_kernel,
        out_shape=(
            jax.ShapeDtypeStruct((bins, 2 * chans, columns), jnp.bfloat16),
            jax.ShapeDtypeStruct((1 + ROUNDS, bins, chans, 2 * chans), jnp.bfloat16),
        ),
        grid=(bins // step,),
        in_specs=[
            pl.BlockSpec((step, chans, columns), lambda i: (i, 0, 0)),
            pl.BlockSpec((bins, chans), lambda i: (0, 0)),
        ],
        out_specs=[
            pl.BlockSpec((step, 2 * chans, columns), lambda i: (i, 0, 0)),
            pl.BlockSpec((1, step, chans, 2 * chans), lambda i: (0, i, 0, 0)),
        ],
        cost_estimate=pl.CostEstimate(
            flops=4 * bins * chans * chans * columns,
            bytes_accessed=2 * bins * chans * (3 * columns + 2 * chans),
            transcendentals=0,
        ),
        compiler_params=pltpu.CompilerParams(vmem_limit_bytes=16 * MIB),
        name="own_products",
    )(spectra, scale)


def start_kernel(devices, chunk, device_ref, partner_ref, spectra, *refs):
    out_ref, case_ref, *outs, held, arrived, left = refs
    copies = []
    begin = 0
    for piece in outs:
        for local in range(0, piece.shape[0], chunk):
            n = len(copies)
            into = pltpu.make_async_copy(
                spectra.at[pl.ds(begin + local, chunk)], held.at[n], arrived.at[n]
            )
            onto = pltpu.make_async_copy(held.at[n], piece.at[pl.ds(local, chunk)], left.at[n])
            copies.append((into, onto))
        begin += piece.shape[0]
    for into, onto in copies:
        into.start()
    for n, (into, onto) in enumerate(copies):
        if n == len(copies) // 2:
            route_kernel(devices, device_ref, partner_ref, out_ref, case_ref)
        into.wait()
        onto.start()
    for into, onto in copies:
        onto.wait()


def starts_of(device, partner, spectra, parts):
    chans, columns = spectra.shape[1:]
    chunk = 1
    count = 2 * sum(parts) // chunk
    anywhere = pl.BlockSpec(memory_space=pl.ANY)
    smem = pl.BlockSpec(memory_space=pltpu.SMEM)
    route, case, *pieces = pl.pallas_call(
        functools.partial(start_kernel, partner.shape[1], chunk),
        out_shape=(
            jax.ShapeDtypeStruct((LISTS + 2 * LIST,), jnp.int32),
            jax.ShapeDtypeStruct((1,), jnp.int32),
            *(jax.ShapeDtypeStruct((2 * part, chans, columns), spectra.dtype) for part in parts),
        ),
        in_specs=[smem, smem, anywhere],
        out_specs=(smem, smem) + (anywhere,) * len(parts),
        scratch_shapes=[
            pltpu.VMEM((count, chunk, chans, columns), spectra.dtype),
            pltpu.SemaphoreType.DMA((count,)),
            pltpu.SemaphoreType.DMA((count,)),
        ],
        compiler_params=pltpu.CompilerParams(vmem_limit_bytes=6 * MIB),
        name="start",
    )(device.reshape(1), partner, spectra)
    return route, case, pieces


def send_kernel(side, start, route, own, sister, near, far, out_ref, held, arrived, left):
    slots, part = held.shape[:2]
    base = LISTS + side * LIST + SEND
    at = route[HALF] * part
    sources = (
        own.at[pl.ds(start + at, part)],
        sister.at[pl.ds(start + at, part)],
        near.at[pl.ds(at, part)],
        far.at[pl.ds(at, part)],
    )
    for s in range(slots):
        for place, source in enumerate(sources):

            @pl.when(route[base + s] == place)
            def _():
                pltpu.make_async_copy(source, held.at[s], arrived.at[s]).start()

    for s in range(slots):
        pltpu.make_async_copy(sources[0], held.at[s], arrived.at[s]).wait()
        pltpu.make_async_copy(held.at[s], out_ref.at[s], left.at[s]).start()
    for s in range(slots):
        pltpu.make_async_copy(held.at[s], out_ref.at[s], left.at[s]).wait()


def sends(side, slots, start, part, route, own, sister, near, far):
    chans, columns = own.shape[1:]
    anywhere = pl.BlockSpec(memory_space=pl.ANY)
    smem = pl.BlockSpec(memory_space=pltpu.SMEM)
    return pl.pallas_call(
        functools.partial(send_kernel, side, start),
        out_shape=jax.ShapeDtypeStruct((slots, part, chans, columns), jnp.bfloat16),
        in_specs=[smem] + [anywhere] * 4,
        out_specs=anywhere,
        scratch_shapes=[
            pltpu.VMEM((slots, part, chans, columns), jnp.bfloat16),
            pltpu.SemaphoreType.DMA((slots,)),
            pltpu.SemaphoreType.DMA((slots,)),
        ],
        cost_estimate=pl.CostEstimate(
            flops=0, bytes_accessed=4 * slots * part * chans * columns, transcendentals=0
        ),
        compiler_params=pltpu.CompilerParams(vmem_limit_bytes=6 * MIB),
        name="send",
    )(route, own, sister, near, far)


def pair_kernel(parts, offset, which, raw, inside, unroll, route, both, sister, *refs):
    out_ref, held, done, done_out, owned, scale, pure, owned_in, held_in, scale_in = refs[-10:]
    if raw:
        scales, refs = refs[0], refs[1:]
    half = route[HALF] if which == TAKE else 1 - route[HALF]
    total = sum(parts)
    sides = []
    for side, part in enumerate(parts):
        if part:
            sides.append((side, part, *refs[:3]))
            refs = refs[3:]

    def place_of(side, r):
        return route[LISTS + side * LIST + which + r]

    def bin_of(j):
        return jnp.where(j < parts[0], half * parts[0] + j, parts[0] + half * parts[1] + j)

    if raw:
        for r in range(ROUNDS):
            source = scales.at[route[OFFSETS + r]]
            pltpu.make_async_copy(source, scale.at[r], scale_in.at[r]).start()

    def fetch(j):
        pltpu.make_async_copy(both.at[offset + bin_of(j)], owned.at[j], owned_in.at[j]).start()
        for side, part, near, far, got in sides:

            @pl.when((j >= parts[0]) == (side == 1))
            def _():
                at = half * part + j - (parts[0] if side else 0)
                for r in range(ROUNDS):
                    place = place_of(side, r)
                    for chosen, source in (
                        (place <= 1, sister.at[bin_of(j)]),
                        (place == 2, near.at[at]),
                        (place == 3, far.at[at]),
                    ):

                        @pl.when(chosen)
                        def _():
                            pltpu.make_async_copy(source, held.at[r, j], held_in.at[r, j]).start()

    if not inside:
        for j in range(AHEAD):
            fetch(jnp.int32(j))

    if raw:
        for r in range(ROUNDS):
            pltpu.make_async_copy(scales.at[0], scale.at[r], scale_in.at[r]).wait()

    def ready(j):
        for side, part, near, far, got in sides:

            @pl.when((j >= parts[0]) == (side == 1))
            def _():
                local = j - (parts[0] if side else 0)
                at = half * part + local
                for r in range(ROUNDS):
                    place = place_of(side, r)

                    @pl.when(place >= 4)
                    def _():
                        held[r, j] = got[place - 4, local]

                    if inside:
                        for chosen, source, where in (
                            (place <= 1, sister, bin_of(j)),
                            (place == 2, near, at),
                            (place == 3, far, at),
                        ):

                            @pl.when(chosen)
                            def _():
                                held[r, j] = source[where]

                    else:

                        @pl.when(place < 4)
                        def _():
                            pltpu.make_async_copy(
                                sister.at[0], held.at[r, j], held_in.at[r, j]
                            ).wait()

        if not inside:
            pltpu.make_async_copy(both.at[0], owned.at[j], owned_in.at[j]).wait()

    def compute(j):
        own = both[bin_of(j)] if inside else owned[j]
        for r in range(ROUNDS):
            other = pure[lax.rem(j, 2), r] if raw else held[r, j]
            multiply(own, other, done, j, r)

    def whiten(j):
        for r in range(ROUNDS):
            rows = column(scale[r, pl.ds(offset + bin_of(j), 1), :])
            white = held[r, j].astype(jnp.float32) * rows
            pure[lax.rem(j, 2), r] = white.astype(jnp.bfloat16)

    def leave(j):
        target = out_ref.at[pl.ds(1, ROUNDS), offset + bin_of(j)]
        return pltpu.make_async_copy(done.at[j], target, done_out.at[j])

    def step(i, carry):
        if not inside:

            @pl.when(i + AHEAD < total)
            def _():
                fetch(i + AHEAD)

        if raw:

            @pl.when(i + 1 < total)
            def _():
                ready(i + 1)

            compute(i)
            whiten(jnp.minimum(i + 1, total - 1))
            leave(i).start()
            return carry
        for k in range(unroll):
            ready(i * unroll + k)
        for k in range(unroll):
            compute(i * unroll + k)
            leave(i * unroll + k).start()
        return carry

    if raw:
        ready(jnp.int32(0))
        whiten(jnp.int32(0))
    lax.fori_loop(0, total // unroll, step, 0)
    for j in range(total):
        leave(j).wait()


def pair_products(
    which, parts, offset, inside, unroll, route, both, sister, scales, pieces, result
):
    chans, columns = sister.shape[1:]
    anywhere = pl.BlockSpec(memory_space=pl.ANY)
    within = pl.BlockSpec(memory_space=pltpu.VMEM)
    place = within if inside else anywhere
    raw = scales is not None
    operands = [route, both, sister]
    in_specs = [pl.BlockSpec(memory_space=pltpu.SMEM), place, place]
    if raw:
        operands.append(scales)
        in_specs.append(anywhere)
    for piece in pieces:
        operands += list(piece)
        in_specs += [place, place, within]
    total = sum(parts)
    fetched = 1 if inside else total
    bins = scales.shape[1] if raw else 8
    return pl.pallas_call(
        lambda *refs: pair_kernel(
            parts, offset, which, raw, inside, unroll, *refs[: len(operands)], *refs[len(operands) + 1 :]
        ),
        out_shape=jax.ShapeDtypeStruct(result.shape, result.dtype),
        in_specs=in_specs + [anywhere],
        out_specs=anywhere,
        scratch_shapes=[
            pltpu.VMEM((ROUNDS, total, chans, columns), jnp.bfloat16),
            pltpu.VMEM((total, ROUNDS, chans, 2 * chans), jnp.bfloat16),
            pltpu.SemaphoreType.DMA((total,)),
            pltpu.VMEM((fetched, 2 * chans, columns), jnp.bfloat16),
            pltpu.VMEM((ROUNDS, bins, chans), jnp.float32),
            pltpu.VMEM((2, ROUNDS, chans if raw else 8, columns), jnp.bfloat16),
            pltpu.SemaphoreType.DMA((total,)),
            pltpu.SemaphoreType.DMA((ROUNDS, total)),
            pltpu.SemaphoreType.DMA((ROUNDS,)),
        ],
        input_output_aliases={len(operands): 0},
        cost_estimate=pl.CostEstimate(
            flops=8 * total * chans * chans * columns,
            bytes_accessed=8 * total * chans * (columns + chans),
            transcendentals=0,
        ),
        compiler_params=pltpu.CompilerParams(vmem_limit_bytes=(16 if inside else 21) * MIB),
    )(*operands, result)


def exchange(slots, pairs, spectra, half_width, route, *pieces):
    ends = [0]
    for parts in pairs:
        ends.append(ends[-1] + 2 * sum(parts))

    def piece_of(values, p, side):
        start = 2 * pairs[p][0] if side else 0
        return values[start : start + 2 * pairs[p][side]]

    def near_of(pieces, p):
        near = [None, None]
        for side, (first, second) in enumerate(SIDES):
            if pairs[p][side]:
                near[side] = swap(pieces[side], first)
        return near

    near = [near_of(pieces, 0)]
    owns = [spectra]
    sisters = [swap(owns[0], CORE)]
    scale = whitening_scale(spectra, half_width)
    for p in range(1, len(pairs)):
        owns.append(whitened(spectra[ends[p] : ends[p + 1]], scale[ends[p] : ends[p + 1]]))
        near.append(near_of([piece_of(owns[p], p, side) for side in (0, 1)], p))
        sisters.append(swap(owns[p], CORE))
    couple = jnp.stack([scale, swap(scale, CORE)])
    scales = [couple]
    for offset in (AXIS_X, AXIS_Y, AXIS_X | AXIS_Y):
        scales.append(swap(couple, offset))
    scales = jnp.concatenate(scales)
    both, result = own_products(spectra, scale)
    far, got = [], []
    for p, parts in enumerate(pairs):
        far.append([None, None])
        got.append([None, None])
        for side, (first, second) in enumerate(SIDES):
            part = parts[side]
            if part:
                far[p][side] = swap(near[p][side], CORE)
                sent = sends(
                    side,
                    slots,
                    2 * parts[0] if side else 0,
                    part,
                    route,
                    owns[p],
                    sisters[p],
                    near[p][side],
                    far[p][side],
                )
                got[p][side] = swap(sent, second)
    for p, parts in enumerate(pairs):
        used = [side for side in (0, 1) if parts[side]]
        shared = {}
        for side in used:
            shared[side] = swap(got[p][side], CORE)
        owned = both[ends[p] : ends[p + 1]] if p else both
        for which, table in ((TAKE, {side: got[p][side] for side in used}), (THEIRS, shared)):
            pieces = [(near[p][side], far[p][side], table[side]) for side in used]
            result = pair_products(
                which,
                parts,
                ends[p],
                p > 0,
                UNROLL[p],
                route,
                owned,
                sisters[p],
                None if p else scales,
                pieces,
                result,
            )
    return result


PAIRS = ((4, 4), (2, 2))
UNROLL = (1, 2)
AHEAD = 3
CASES = [(2, PAIRS), (3, PAIRS), (4, PAIRS)]


def paired_body(spectra, half_width, partner):
    device = lax.axis_index("chan").astype(jnp.int32)
    route, case, pieces = starts_of(device, partner, spectra, PAIRS[0])
    choices = [functools.partial(exchange, slots, pairs) for slots, pairs in CASES]
    return lax.switch(case.reshape(()), choices, spectra, half_width, route, *pieces)


def solution(mesh):
    placed = (P("band", "chan", None), P("chan"), P())
    paired = mesh.shape["chan"] == 8
    return jax.shard_map(
        paired_body if paired else general_body,
        mesh=mesh,
        in_specs=placed,
        out_specs=P(None, "band", "chan", None),
        check_vma=False,
    )
```
